512 devices in a mesh: gx: 8 (over y), gy: 4 (over x), gz: 16 (over z, core).
Axes of the slice: x: 4, y: 8, z: 8, core: 2. Of those that a mesh axis runs over, the one named last changes fastest.
Arguments:
- fields: float32 [4, 512, 256, 512], P(None, 'gz', 'gx', 'gy'), may hold values from -6 to 6
- material: int32 [512, 256, 512], P('gz', 'gx', 'gy'), may hold values from 0 to 15
- depth_order: int32 [16], replicated, may hold values from 0 to 15, each once
- table: float32 [4, 16], replicated, may hold values from 0.2 to 2
Outputs:
- image: float32 [4, 256, 512], P(None, ('gx', 'gz'), 'gy')
The draws below stay inside these ranges and needn't reach their ends.
Inputs may be any that keep to these rules, and one draw needn't show every extreme that they name: `depth_order`: a permutation: each brick layer along gz gets a distinct rank, 0 nearest the viewer.
All inputs are finite; a program needn't handle non-finite values.
Results may differ from the reference program's by a relative error of at most 0.0003.
Values sent between devices are 32-bit elements; how exact they have to be, the bound alone decides.
A program may use at most 64 MiB of HBM per device.

```python
import jax
import jax.numpy as jnp
from jax import lax

BX = 32
BY = 128
BZ = 32
MATS = 16
NX = 256
NY = 512
NZ = 512
N_GX = 8
N_GY = 4
N_GZ = 16


def with_ends(values, key, least, top_value):
    longest = values.shape.index(max(values.shape))
    spots = []
    for shift in (0, 1):
        where = [jax.random.randint(jax.random.fold_in(key, axis), (), 0, length) for axis, length in enumerate(values.shape)]
        where[longest] = (where[longest] + shift) % values.shape[longest]
        spots.append(tuple(where))
    return values.at[spots[0]].set(least).at[spots[1]].set(top_value)


def levels(own_key, dims, pieces, low, largest):
    factor_of = 1.0
    for position, shards_of in pieces:
        draws = jax.random.uniform(jax.random.fold_in(jax.random.fold_in(own_key, 6), position), (shards_of,), jnp.float32, low / len(pieces), largest / len(pieces))
        factor_of = factor_of * jnp.repeat(jnp.exp(draws), dims[position] // shards_of).reshape((-1,) + (1,) * (len(dims) - 1 - position))
    return factor_of


def noise(rng, extent, deviation, limit, split=(), kind=jnp.bfloat16):
    gain = levels(rng, extent, split, -0.22, 0.18) if split else 1.0
    drawn = jax.random.normal(rng, extent, jnp.float32) * deviation * gain
    return jnp.minimum(jnp.maximum(drawn, -limit), limit).astype(kind)


def setup_inputs(seed: int = 0) -> dict:
    key_of = jax.random.split(jax.random.key(seed), 5)
    fields = noise(key_of[0], (4, NZ, NX, NY), 1.0, 6.0, ((1, 16), (2, 8), (3, 4)), jnp.float32)
    material = with_ends(jax.random.randint(key_of[1], (NZ, NX, NY), 0, MATS), jax.random.fold_in(key_of[1], 1), 0, MATS - 1).astype(jnp.int32)
    depth_order = jax.random.permutation(key_of[2], N_GZ).astype(jnp.int32)
    table = jnp.clip(jax.random.uniform(key_of[3], (4, MATS), jnp.float32, 0.2, 2.0), 0.2, 2.0)
    return {"fields": fields, "material": material, "depth_order": depth_order, "table": table}


ambient = 0.3
diffuse = 1.2
grad_floor = 0.0025
light_z = 2.0 / 3.0
light_x = 1.0 / 3.0
light_y = 2.0 / 3.0

def blur_axis(values, which):
    length = values.shape[which]
    lower = lax.slice_in_dim(values, 0, length - 2, axis=which)
    middle = lax.slice_in_dim(values, 1, length - 1, axis=which)
    upper = lax.slice_in_dim(values, 2, length, axis=which)
    return (lower + 2.0 * middle + upper) * 0.25

def slope_axis(values, which):
    length = values.shape[which]
    lower = lax.slice_in_dim(values, 0, length - 2, axis=which)
    upper = lax.slice_in_dim(values, 2, length, axis=which)
    return (upper - lower) * 0.5

def smooth_all(values):
    for which in (1, 2, 3):
        values = blur_axis(values, which)
    return values

def shade_brick(smoothed, density, material, table, depth_total):
    grad_z = blur_axis(blur_axis(slope_axis(density, 0), 1), 2)
    grad_x = blur_axis(blur_axis(slope_axis(density, 1), 0), 2)
    grad_y = blur_axis(blur_axis(slope_axis(density, 2), 0), 1)
    facing = jnp.abs(light_z * grad_z + light_x * grad_x + light_y * grad_y)
    length = jnp.sqrt(grad_z * grad_z + grad_x * grad_x + grad_y * grad_y + grad_floor)
    shading = ambient + diffuse * facing / length
    entries = table.shape[1]
    onehot = (material[None] == jnp.arange(entries, dtype=jnp.int32)[:, None, None, None]).astype(jnp.float32)
    looked = jnp.einsum('cm,mzxy->czxy', table, onehot, precision=lax.Precision.HIGHEST)
    extinct = looked[3] * jax.nn.softplus(3.0 * smoothed[0]) * (2.0 / depth_total)
    colour = looked[:3] * shading[None] * (0.5 + jax.nn.sigmoid(2.0 * smoothed[1:]))
    ahead = jnp.cumsum(extinct, axis=0) - extinct
    weight = jnp.exp(-ahead) * -jnp.expm1(-extinct)
    return (lax.optimization_barrier(jnp.sum(weight[None] * colour, axis=1)), lax.optimization_barrier(jnp.sum(extinct, axis=0)))

def reference(fields, material, depth_order, table):
    depth_total = BZ * N_GZ
    width_total = BX * N_GX
    height_total = BY * N_GY
    padded = jnp.pad(fields, ((0, 0), (2, 2), (2, 2), (2, 2)))

    def one_brick(brick):
        start = brick * BZ
        slab_part = lax.dynamic_slice_in_dim(padded, start, BZ + 4, axis=1)
        smoothed = smooth_all(slab_part)
        zpos = start - 1 + jnp.arange(BZ + 2, dtype=jnp.int32)
        xpos = jnp.arange(width_total + 2, dtype=jnp.int32) - 1
        ypos = jnp.arange(height_total + 2, dtype=jnp.int32) - 1
        inside = ((zpos >= 0) & (zpos < depth_total))[:, None, None] & ((xpos >= 0) & (xpos < width_total))[None, :, None] & ((ypos >= 0) & (ypos < height_total))[None, None, :]
        density = jnp.where(inside, smoothed[0], jnp.zeros_like(smoothed[0]))
        local_ids = lax.dynamic_slice_in_dim(material, start, BZ, axis=0)
        return shade_brick(smoothed[:, 1:-1, 1:-1, 1:-1], density, local_ids, table, depth_total)
    colours, depths = lax.map(one_brick, jnp.arange(N_GZ, dtype=jnp.int32))
    before = (depth_order[None, :] < depth_order[:, None]).astype(jnp.float32)
    prior = jnp.einsum('gh,hxy->gxy', before, depths, precision=lax.Precision.HIGHEST)
    colour = lax.optimization_barrier(jnp.sum(jnp.exp(-prior)[:, None] * colours, axis=0))
    total = lax.optimization_barrier(jnp.sum(depths, axis=0))
    return jnp.concatenate([colour, (-jnp.expm1(-total))[None]], axis=0)
```

```python
import math

import jax
import jax.numpy as jnp
from jax import lax
from jax.experimental import pallas as pl
from jax.experimental.pallas import tpu as pltpu
from jax.sharding import PartitionSpec as P

MESH = pl.DeviceIdType.MESH
f32 = jnp.float32

BZ = 32
BX = 32
ROW0 = 8
ROWS = 48

OFFSETS = [
    (dz, dx, dy)
    for dz in (-1, 0, 1)
    for dx in (-1, 0, 1)
    for dy in (-1, 0, 1)
    if (dz, dx, dy) != (0, 0, 0)
]


def z_range(dz, width):
    if dz == 1:
        return pl.ds(BZ - width, width), pl.ds(2 - width, width)
    if dz == -1:
        return pl.ds(0, width), pl.ds(2 + BZ, width)
    return pl.ds(0, BZ), pl.ds(2, BZ)


def x_range(dx, width):
    if dx == 1:
        return pl.ds(BX - width, width), pl.ds(ROW0 - width, width)
    if dx == -1:
        return pl.ds(0, width), pl.ds(ROW0 + BX, width)
    return pl.ds(0, BX), pl.ds(ROW0, BX)


def blur3(cells):
    pairs = [a + b for a, b in zip(cells[:-1], cells[1:])]
    return [a + b for a, b in zip(pairs[:-1], pairs[1:])]


def kernel(
    fields, material, order_hbm, table_hbm, out,
    V, M, S, R, WD, WDE, WF, G, D, SM, LK, TB, table, order, SB, RB,
    load_sem, send_sem, recv_sem, a2a_send, a2a_recv,
):
    gz, gx, gy = lax.axis_index("gz"), lax.axis_index("gx"), lax.axis_index("gy")
    nz, nx, ny = lax.axis_size("gz"), lax.axis_size("gx"), lax.axis_size("gy")

    def there(dz, dx, dy):
        ok = None
        for pos, d, n in ((gz, dz, nz), (gx, dx, nx), (gy, dy, ny)):
            if d == 0:
                continue
            this = pos < n - 1 if d == 1 else pos > 0
            ok = this if ok is None else jnp.logical_and(ok, this)
        return ok

    loads = [
        pltpu.make_async_copy(
            fields.at[f], V.at[f, pl.ds(2, BZ), pl.ds(ROW0, BX)], load_sem.at[f]
        )
        for f in range(4)
    ]
    load_m = pltpu.make_async_copy(material, M, load_sem.at[4])
    load_t = pltpu.make_async_copy(table_hbm, table, load_sem.at[5])
    load_o = pltpu.make_async_copy(order_hbm, order, load_sem.at[6])
    for c in loads:
        c.start()
    load_m.start()
    load_t.start()
    load_o.start()

    barrier = pltpu.get_barrier_semaphore()
    for k in range(2, nz):
        for peer, ok in ((gz + k, gz + k < nz), (gz - k, gz - k >= 0)):
            @pl.when(ok)
            def _():
                pl.semaphore_signal(
                    barrier, inc=1, device_id={"gz": peer}, device_id_type=MESH
                )
    for dz, dx, dy in OFFSETS:
        @pl.when(there(dz, dx, dy))
        def _():
            pl.semaphore_signal(
                barrier,
                inc=1,
                device_id={"gz": gz + dz, "gx": gx + dx, "gy": gy + dy},
                device_id_type=MESH,
            )

    def span(pos, n):
        return 1 + (pos > 0).astype(jnp.int32) + (pos < n - 1).astype(jnp.int32)

    expected = span(gz, nz) * span(gx, nx) * span(gy, ny) - span(gz, nz) + nz - 1

    lane = lax.broadcasted_iota(jnp.int32, (8, 128), 1)
    sub = lax.broadcasted_iota(jnp.int32, (8, 128), 0)
    lane4 = lane % 4
    lane_z = lane // 4

    acc = [[jnp.zeros((8, 128), f32)] * 4 for _ in range(4)]
    shift0 = (2, 3, 3, 1)
    for f in range(4):
        loads[f].wait()
        for z in range(BZ):
            mask = lane_z == z
            for i in range(4):
                tile = V[f, z + 2, ROW0 + 8 * i : ROW0 + 8 * i + 8, :]
                moved = pltpu.roll(tile, (4 * z + shift0[f]) % 128, 1)
                acc[f][i] = jnp.where(mask, moved, acc[f][i])
    for i in range(4):
        ad, a1, a2, b = (acc[f][i] for f in range(4))
        front = jnp.where(lane4 < 2, ad, jnp.where(lane4 == 2, a1, pltpu.roll(a2, 1, 1)))
        back = jnp.where(
            lane4 >= 2, ad, jnp.where(lane4 == 0, pltpu.roll(a1, 125, 1), pltpu.roll(a2, 126, 1))
        )
        for s, a in ((0, front), (1, back)):
            rows = pl.ds(8 * i, 8)
            S[s, 0, rows, :] = a
            S[s, 1, rows, :] = b
            S[s, 2, rows, :] = jnp.where(
                lane < 4,
                pltpu.roll(a, 4, 1),
                jnp.where(lane < 8, pltpu.roll(a, 12, 1), pltpu.roll(b, 12, 1)),
            )
            S[s, 3, rows, :] = jnp.where(
                lane >= 124,
                pltpu.roll(a, 124, 1),
                jnp.where(lane >= 120, pltpu.roll(a, 116, 1), pltpu.roll(b, 116, 1)),
            )

    def copies(n, dz, dx, dy):
        device = {"gz": gz + dz, "gx": gx + dx, "gy": gy + dy}

        def make(src, dst, k):
            return pltpu.make_async_remote_copy(
                src_ref=src,
                dst_ref=dst,
                send_sem=send_sem.at[n, k],
                recv_sem=recv_sem.at[n, k],
                device_id=device,
                device_id_type=MESH,
            )

        xs2, xd2 = x_range(dx, 2)
        if dy == 0:
            zs2, zd2 = z_range(dz, 2)
            zs1, zd1 = z_range(dz, 1)
            xs1, xd1 = x_range(dx, 1)
            return [
                make(fields.at[0, zs2, xs2], V.at[0, zd2, xd2], 0),
                make(fields.at[pl.ds(1, 3), zs1, xs1], V.at[pl.ds(1, 3), zd1, xd1], 1),
            ]
        side = 0 if dy == 1 else 1
        kinds = {0: pl.ds(0, 2), 1: pl.ds(2, 1), -1: pl.ds(3, 1)}[dz]
        return [make(S.at[side, kinds, xs2], R.at[side, kinds, xd2], 0)]

    pl.semaphore_wait(barrier, expected)
    for n, (dz, dx, dy) in enumerate(OFFSETS):
        @pl.when(there(dz, dx, dy))
        def _():
            for c in copies(n, dz, dx, dy):
                c.start()

    zrow = jnp.zeros((2, 128), f32)

    @pl.when(gx == 0)
    def _():
        for s in range(2):
            for k in range(4):
                R[s, k, ROW0 - 2 : ROW0, :] = zrow

        @pl.loop(0, BZ + 4)
        def _(z):
            for f in range(4):
                V[f, z, ROW0 - 2 : ROW0, :] = zrow

    @pl.when(gx == nx - 1)
    def _():
        for s in range(2):
            for k in range(4):
                R[s, k, ROW0 + BX : ROW0 + BX + 2, :] = zrow

        @pl.loop(0, BZ + 4)
        def _(z):
            for f in range(4):
                V[f, z, ROW0 + BX : ROW0 + BX + 2, :] = zrow

    zrows = jnp.zeros((BX + 4, 128), f32)

    def clear_planes(planes, kind):
        for s in range(2):
            R[s, kind, ROW0 - 2 : ROW0 + BX + 2, :] = zrows
        for f in range(4):
            for z in planes:
                V[f, z, ROW0 - 2 : ROW0 + BX + 2, :] = zrows

    @pl.when(gz == 0)
    def _():
        clear_planes((0, 1), 2)

    @pl.when(gz == nz - 1)
    def _():
        clear_planes((BZ + 2, BZ + 3), 3)

    for s, edge in ((0, 0), (1, ny - 1)):
        @pl.when(gy == edge)
        def _():
            for k in range(4):
                R[s, k, ROW0 - 2 : ROW0 + BX + 2, :] = zrows

    load_m.wait()
    load_t.wait()
    load_o.wait()
    depth_total = BZ * nz
    TB[...] = jnp.zeros(TB.shape, f32)
    for c in range(4):
        entries = jnp.broadcast_to(table[c : c + 1, :], (8, table.shape[1]))
        TB[c, :, 0 : table.shape[1]] = entries * (2.0 / depth_total) if c == 3 else entries

    @pl.loop(0, BZ)
    def _(z):
        tables = [TB[c] for c in range(4)]
        for j in range(4):
            index = M[z, pl.ds(j, 8, stride=4), :]
            for c in range(4):
                LK[z, c, j] = jnp.take_along_axis(tables[c], index, axis=1)

    for n, (dz, dx, dy) in enumerate(OFFSETS):
        @pl.when(there(-dz, -dx, -dy))
        def _():
            for c in copies(n, dz, dx, dy):
                c.wait_recv()

    on = lambda cond: cond.astype(f32)
    low_x = jnp.where(sub == 0, on(gx > 0), 1.0)
    high_x = jnp.where(sub == 7, on(gx < nx - 1), 1.0)
    low_z, high_z = on(gz > 0), on(gz < nz - 1)
    y_first = jnp.where(lane == 0, on(gy == 0), 0.0)
    y_last = jnp.where(lane == 127, on(gy == ny - 1), 0.0)
    six = 6.0 - y_first - y_last
    edge_sign = y_first - y_last

    def x_mask(cells):
        return [cells[0] * low_x] + cells[1:5] + [cells[5] * high_x]

    def packed(s, k, js):
        return [R[s, k, pl.ds(ROW0 + j, 8, stride=4), :] for j in js]

    js = range(-2, 6)
    near = [packed(0, k, js) for k in range(4)]
    far = [packed(1, k, js) for k in range(4)]
    dens = [
        blur3([jnp.where(lane4 < 2, a, b) for a, b in zip(near[k], far[k])]) for k in (0, 2, 3)
    ]
    for j in range(6):
        u, lo, hi = dens[0][j], dens[1][j], dens[2][j]
        below = jnp.where(lane < 4, lo, pltpu.roll(u, 4, 1))
        above = jnp.where(lane >= 124, hi, pltpu.roll(u, 124, 1))
        mask = low_x if j == 0 else high_x if j == 5 else None
        w = below + 2.0 * u + above
        w_lo = (pltpu.roll(lo, 124, 1) + 2.0 * lo + u) * low_z
        w_hi = (pltpu.roll(hi, 4, 1) + 2.0 * hi + u) * high_z
        if mask is not None:
            w, w_lo, w_hi = w * mask, w_lo * mask, w_hi * mask
        WD[j] = w
        WDE[0, j] = w_lo
        WDE[1, j] = w_hi

    def pair(f, k):
        cells = []
        for a, b in zip(near[k][1:7], far[k][1:7]):
            if f == 1:
                cells.append(jnp.where(lane4 == 2, a, pltpu.roll(b, 3, 1)))
            elif f == 2:
                cells.append(jnp.where(lane4 == 2, pltpu.roll(a, 127, 1), pltpu.roll(b, 2, 1)))
            else:
                cells.append(jnp.where(lane4 == 0, a, b))
        return blur3(cells)

    for f in (1, 2, 3):
        main = pair(f, 1 if f == 3 else 0)
        lo, hi = pair(f, 2), pair(f, 3)
        for j in range(4):
            lo_j, hi_j = lo[j], hi[j]
            if f == 3:
                lo_j, hi_j = pltpu.roll(lo_j, 120, 1), pltpu.roll(hi_j, 8, 1)
            below = jnp.where(lane < 4, lo_j, pltpu.roll(main[j], 4, 1))
            above = jnp.where(lane >= 124, hi_j, pltpu.roll(main[j], 124, 1))
            WF[f - 1, j] = below + 2.0 * main[j] + above

    first, last = lane == 0, lane == 127
    first2, last2 = lane <= 1, lane >= 126

    def x_blur(f, plane, js):
        return blur3([V[f, plane, pl.ds(ROW0 + j, 8, stride=4), :] for j in js])

    def density_plane(z, w, edges):
        by, sy = [], []
        for j in range(6):
            a, e = w[j], edges[j]
            l1 = pltpu.roll(jnp.where(last, e, a), 1, 1)
            l2 = pltpu.roll(jnp.where(last2, e, a), 2, 1)
            r1 = pltpu.roll(jnp.where(first, e, a), 127, 1)
            r2 = pltpu.roll(jnp.where(first2, e, a), 126, 1)
            p1, m1 = l1 + r1, r1 - l1
            by.append((l2 + r2) + 4.0 * p1 + a * six)
            sy.append((r2 - l2) + 2.0 * m1 + a * edge_sign)
            if 1 <= j <= 4:
                D[z + 1, j - 1] = p1 + 2.0 * a
        bb = blur3(by)
        bs = blur3(sy)
        for j in range(4):
            G[0, z + 1, j] = bb[j]
            G[1, z + 1, j] = by[j + 2] - by[j]
            G[2, z + 1, j] = bs[j]

    def blend(a, b, c):
        return [p + 2.0 * q + r for p, q, r in zip(a, b, c)]

    u0 = x_blur(0, 0, js)
    u1 = x_blur(0, 1, js)
    u2 = x_blur(0, 2, js)
    w = x_mask([x * low_z for x in blend(u0, u1, u2)])
    density_plane(-1, w, [pltpu.roll(WDE[0, j], 126, 1) for j in range(6)])

    def density_step(z, carry):
        before, here = carry[:6], carry[6:]
        after = x_blur(0, z + 3, js)
        w = x_mask(blend(before, here, after))
        amount = lax.rem(126 - 4 * z + 128, 128)
        density_plane(z, w, [pltpu.roll(WD[j], amount, 1) for j in range(6)])
        return tuple(here) + tuple(after)

    def density_two(i, carry):
        return density_step(2 * i + 1, density_step(2 * i, carry))

    carry = lax.fori_loop(0, BZ // 2, density_two, tuple(u1) + tuple(u2))
    u3 = x_blur(0, BZ + 3, js)
    w = x_mask([x * high_z for x in blend(carry[:6], carry[6:], u3)])
    density_plane(BZ, w, [pltpu.roll(WDE[1, j], 2, 1) for j in range(6)])

    js1 = range(-1, 5)

    def field_step(z, carry):
        new = []
        for f in (1, 2, 3):
            before = carry[8 * (f - 1) : 8 * (f - 1) + 4]
            here = carry[8 * (f - 1) + 4 : 8 * f]
            after = x_blur(f, z + 3, js1)
            w = blend(before, here, after)
            amount = lax.rem((127 if f == 3 else 125) - 4 * z + 128, 128)
            for j in range(4):
                e = pltpu.roll(WF[f - 1, j], amount, 1)
                l1 = pltpu.roll(jnp.where(last, e, w[j]), 1, 1)
                r1 = pltpu.roll(jnp.where(first, e, w[j]), 127, 1)
                SM[z, f - 1, j] = l1 + r1 + 2.0 * w[j]
            new += list(here) + list(after)
        return tuple(new)

    def field_two(i, carry):
        return field_step(2 * i + 1, field_step(2 * i, carry))

    carry = []
    for f in (1, 2, 3):
        carry += x_blur(f, 1, js1) + x_blur(f, 2, js1)
    lax.fori_loop(0, BZ // 2, field_two, tuple(carry))

    to_exp2 = 3.0 / (64.0 * math.log(2.0))

    def shade_step(z, carry):
        light, depth, red, green, blue = (list(carry[4 * k : 4 * k + 4]) for k in range(5))
        colour = [red, green, blue]
        for j in range(4):
            g_z = G[0, z + 2, j] - G[0, z, j]
            g_x = G[1, z, j] + 2.0 * G[1, z + 1, j] + G[1, z + 2, j]
            g_y = G[2, z, j] + 2.0 * G[2, z + 1, j] + G[2, z + 2, j]
            facing = jnp.abs(2.0 * (g_z + g_y) + g_x)
            norm = g_z * g_z + g_x * g_x + g_y * g_y + 0.0025 * 2048.0 * 2048.0
            shading = 0.3 + 0.4 * facing * lax.rsqrt(norm)
            grown = jnp.exp2(D[z + 1, j] * to_exp2)
            soft = jnp.where(
                grown < 1.0 / 128.0,
                grown * (1.0 + grown * (-0.5 + grown * (1.0 / 3.0))),
                jnp.log(1.0 + grown),
            )
            e = LK[z, 3, j] * soft
            taken = e * (
                1.0 + e * (-0.5 + e * (1.0 / 6.0 + e * (-1.0 / 24.0 + e * (1.0 / 120.0))))
            )
            weight = light[j] * taken
            light[j] = light[j] - weight
            depth[j] = depth[j] + e
            lit = weight * shading
            for c in range(3):
                tone = 1.0 + 0.5 * jnp.tanh(SM[z, c, j] * (1.0 / 64.0))
                colour[c][j] = colour[c][j] + lit * (LK[z, c, j] * tone)
        return tuple(light + depth + colour[0] + colour[1] + colour[2])

    def shade_two(i, carry):
        return shade_step(2 * i + 1, shade_step(2 * i, carry))

    zero = jnp.zeros((8, 128), f32)
    final = lax.fori_loop(
        0, BZ // 2, shade_two, tuple([jnp.ones((8, 128), f32)] * 4 + [zero] * 16)
    )

    for c, k in ((0, 2), (1, 3), (2, 4), (3, 1)):
        for j in range(4):
            SB[pl.ds(8 * (j // 2) + 2 * c + j % 2, 8, stride=16), :] = final[4 * k + j]

    def to_peer(k):
        peer = lax.rem(gz + k, nz)
        return pltpu.make_async_remote_copy(
            src_ref=SB.at[pl.ds(pl.multiple_of(peer * 8, 8), 8)],
            dst_ref=RB.at[pl.ds(pl.multiple_of(gz * 8, 8), 8)],
            send_sem=a2a_send.at[k],
            recv_sem=a2a_recv.at[k],
            device_id={"gz": peer},
            device_id_type=MESH,
        )

    far_first = sorted(range(1, nz), key=lambda k: (-min(k, nz - k), k))
    for k in far_first:
        to_peer(k).start()
    own = pl.ds(pl.multiple_of(gz * 8, 8), 8)
    RB[own, :] = SB[own, :]
    for n, (dz, dx, dy) in enumerate(OFFSETS):
        @pl.when(there(dz, dx, dy))
        def _():
            for c in copies(n, dz, dx, dy):
                c.wait_send()
    for k in reversed(far_first):
        to_peer(k).wait_recv()

    parts = [RB[8 * b : 8 * b + 8, :] for b in range(nz)]
    depths = []
    for part in parts:
        d = jnp.where(sub >= 6, part, 0.0)
        d = d + pltpu.roll(d, 4, 0)
        depths.append(d + pltpu.roll(d, 2, 0))
    total = depths[0]
    for d in depths[1:]:
        total = total + d
    image = zero
    for b in range(nz):
        prior = zero
        for o in range(nz):
            if o != b:
                prior = prior + jnp.where(order[o] < order[b], depths[o], 0.0)
        image = image + jnp.exp(-prior) * parts[b]
    small = total * (
        1.0 + total * (-0.5 + total * (1.0 / 6.0 + total * (-1.0 / 24.0 + total * (1.0 / 120.0))))
    )
    opacity = jnp.where(total < 0.125, small, 1.0 - jnp.exp(-total))
    image = jnp.where(sub >= 6, opacity, image)
    for c in range(4):
        out[c] = image[2 * c : 2 * c + 2, :]
    for k in far_first:
        to_peer(k).wait_send()


def on_device(fields, material, depth_order, table):
    vmem = lambda *shape: pltpu.VMEM(shape, f32)
    dma = pltpu.SemaphoreType.DMA
    count = len(OFFSETS)
    return pl.pallas_call(
        kernel,
        out_shape=jax.ShapeDtypeStruct((4, 2, 128), f32),
        in_specs=[pl.BlockSpec(memory_space=pl.ANY)] * 4,
        out_specs=pl.BlockSpec(memory_space=pltpu.VMEM),
        scratch_shapes=[
            vmem(4, BZ + 4, ROWS, 128),
            pltpu.VMEM((BZ, BX, 128), jnp.int32),
            vmem(2, 4, BX, 128),
            vmem(2, 4, ROWS, 128),
            vmem(6, 8, 128),
            vmem(2, 6, 8, 128),
            vmem(3, 4, 8, 128),
            vmem(3, BZ + 2, 4, 8, 128),
            vmem(BZ + 2, 4, 8, 128),
            vmem(BZ, 3, 4, 8, 128),
            vmem(BZ, 4, 4, 8, 128),
            vmem(4, 8, 128),
            vmem(4, 16),
            pltpu.SMEM((16,), jnp.int32),
            vmem(128, 128),
            vmem(128, 128),
            dma((7,)),
            dma((count, 2)),
            dma((count, 2)),
            dma((16,)),
            dma((16,)),
        ],
        compiler_params=pltpu.CompilerParams(collective_id=0, has_side_effects=True),
    )(fields, material, depth_order, table)


def solution(mesh):
    return jax.shard_map(
        on_device,
        mesh=mesh,
        in_specs=(P(None, "gz", "gx", "gy"), P("gz", "gx", "gy"), P(), P()),
        out_specs=P(None, ("gx", "gz"), "gy"),
        check_vma=False,
    )
```

```python
import math

import jax
import jax.numpy as jnp
from jax import lax
from jax.experimental import pallas as pl
from jax.experimental.pallas import tpu as pltpu
from jax.sharding import PartitionSpec as P

MESH = pl.DeviceIdType.MESH
f32 = jnp.float32

BZ = 32
BX = 32
ROW0 = 8
ROWS = 48

OFFSETS = [
    (dz, dx, dy)
    for dz in (-1, 0, 1)
    for dx in (-1, 0, 1)
    for dy in (-1, 0, 1)
    if (dz, dx, dy) != (0, 0, 0)
]
OFFSETS.sort(key=lambda o: -abs(o[0]) - abs(o[1]) - abs(o[2]))


def z_range(dz, width):
    if dz == 1:
        return pl.ds(BZ - width, width), pl.ds(2 - width, width)
    if dz == -1:
        return pl.ds(0, width), pl.ds(2 + BZ, width)
    return pl.ds(0, BZ), pl.ds(2, BZ)


def x_range(dx, width):
    if dx == 1:
        return pl.ds(BX - width, width), pl.ds(ROW0 - width, width)
    if dx == -1:
        return pl.ds(0, width), pl.ds(ROW0 + BX, width)
    return pl.ds(0, BX), pl.ds(ROW0, BX)


def blur3(cells):
    pairs = [a + b for a, b in zip(cells[:-1], cells[1:])]
    return [a + b for a, b in zip(pairs[:-1], pairs[1:])]


def kernel(
    fields, material, order_hbm, table_hbm, out,
    V, M, S, R, WD, WDE, WF, G, D, SM, LK, TB, table, order, SB, RB,
    load_sem, send_sem, recv_sem, a2a_send, a2a_recv, greeted,
):
    gz, gx, gy = lax.axis_index("gz"), lax.axis_index("gx"), lax.axis_index("gy")
    nz, nx, ny = lax.axis_size("gz"), lax.axis_size("gx"), lax.axis_size("gy")

    def there(dz, dx, dy):
        ok = None
        for pos, d, n in ((gz, dz, nz), (gx, dx, nx), (gy, dy, ny)):
            if d == 0:
                continue
            this = pos < n - 1 if d == 1 else pos > 0
            ok = this if ok is None else jnp.logical_and(ok, this)
        return ok

    loads = [
        pltpu.make_async_copy(
            fields.at[f], V.at[f, pl.ds(2, BZ), pl.ds(ROW0, BX)], load_sem.at[f]
        )
        for f in range(4)
    ]
    load_m = pltpu.make_async_copy(material, M, load_sem.at[4])
    load_t = pltpu.make_async_copy(table_hbm, table, load_sem.at[5])
    load_o = pltpu.make_async_copy(order_hbm, order, load_sem.at[6])
    for c in loads:
        c.start()
    load_m.start()
    load_t.start()
    load_o.start()

    barrier = pltpu.get_barrier_semaphore()
    for dz, dx, dy in OFFSETS:
        @pl.when(there(dz, dx, dy))
        def _():
            pl.semaphore_signal(
                barrier,
                inc=1,
                device_id={"gz": gz + dz, "gx": gx + dx, "gy": gy + dy},
                device_id_type=MESH,
            )

    at_end = jnp.logical_or(gz == 0, gz == nz - 1)

    @pl.when(at_end)
    def _():
        pl.semaphore_signal(
            barrier, inc=1, device_id={"gz": nz - 1 - gz}, device_id_type=MESH
        )

    def greet(k):
        for step in (1 << k, nz - (1 << k)):
            pl.semaphore_signal(
                greeted.at[k], inc=1, device_id={"gz": lax.rem(gz + step, nz)}, device_id_type=MESH
            )

    def span(pos, n):
        return 1 + (pos > 0).astype(jnp.int32) + (pos < n - 1).astype(jnp.int32)

    expected = span(gz, nz) * span(gx, nx) * span(gy, ny) - 1 + at_end.astype(jnp.int32)

    lane = lax.broadcasted_iota(jnp.int32, (8, 128), 1)
    sub = lax.broadcasted_iota(jnp.int32, (8, 128), 0)
    lane4 = lane % 4
    lane_z = lane // 4

    acc = [[jnp.zeros((8, 128), f32)] * 4 for _ in range(4)]
    shift0 = (2, 3, 3, 1)
    for f in range(4):
        loads[f].wait()
        for z in range(BZ):
            mask = lane_z == z
            for i in range(4):
                tile = V[f, z + 2, ROW0 + 8 * i : ROW0 + 8 * i + 8, :]
                moved = pltpu.roll(tile, (4 * z + shift0[f]) % 128, 1)
                acc[f][i] = jnp.where(mask, moved, acc[f][i])
    for i in range(4):
        ad, a1, a2, b = (acc[f][i] for f in range(4))
        front = jnp.where(lane4 < 2, ad, jnp.where(lane4 == 2, a1, pltpu.roll(a2, 1, 1)))
        back = jnp.where(
            lane4 >= 2, ad, jnp.where(lane4 == 0, pltpu.roll(a1, 125, 1), pltpu.roll(a2, 126, 1))
        )
        for s, a in ((0, front), (1, back)):
            rows = pl.ds(8 * i, 8)
            S[s, 0, rows, :] = a
            S[s, 1, rows, :] = b
            S[s, 2, rows, :] = jnp.where(
                lane < 4,
                pltpu.roll(a, 4, 1),
                jnp.where(lane < 8, pltpu.roll(a, 12, 1), pltpu.roll(b, 12, 1)),
            )
            S[s, 3, rows, :] = jnp.where(
                lane >= 124,
                pltpu.roll(a, 124, 1),
                jnp.where(lane >= 120, pltpu.roll(a, 116, 1), pltpu.roll(b, 116, 1)),
            )

    def copies(n, dz, dx, dy):
        device = {"gz": gz + dz, "gx": gx + dx, "gy": gy + dy}

        def make(src, dst, k):
            return pltpu.make_async_remote_copy(
                src_ref=src,
                dst_ref=dst,
                send_sem=send_sem.at[n, k],
                recv_sem=recv_sem.at[n, k],
                device_id=device,
                device_id_type=MESH,
            )

        xs2, xd2 = x_range(dx, 2)
        if dy == 0:
            zs2, zd2 = z_range(dz, 2)
            zs1, zd1 = z_range(dz, 1)
            xs1, xd1 = x_range(dx, 1)
            return [
                make(fields.at[0, zs2, xs2], V.at[0, zd2, xd2], 0),
                make(fields.at[pl.ds(1, 3), zs1, xs1], V.at[pl.ds(1, 3), zd1, xd1], 1),
            ]
        side = 0 if dy == 1 else 1
        kinds = {0: pl.ds(0, 2), 1: pl.ds(2, 1), -1: pl.ds(3, 1)}[dz]
        return [make(S.at[side, kinds, xs2], R.at[side, kinds, xd2], 0)]

    pl.semaphore_wait(barrier, expected)
    for n, (dz, dx, dy) in enumerate(OFFSETS):
        @pl.when(there(dz, dx, dy))
        def _():
            for c in copies(n, dz, dx, dy):
                c.start()

    greet(0)

    zrow = jnp.zeros((2, 128), f32)

    @pl.when(gx == 0)
    def _():
        for s in range(2):
            for k in range(4):
                R[s, k, ROW0 - 2 : ROW0, :] = zrow

        @pl.loop(0, BZ + 4)
        def _(z):
            for f in range(4):
                V[f, z, ROW0 - 2 : ROW0, :] = zrow

    @pl.when(gx == nx - 1)
    def _():
        for s in range(2):
            for k in range(4):
                R[s, k, ROW0 + BX : ROW0 + BX + 2, :] = zrow

        @pl.loop(0, BZ + 4)
        def _(z):
            for f in range(4):
                V[f, z, ROW0 + BX : ROW0 + BX + 2, :] = zrow

    zrows = jnp.zeros((BX + 4, 128), f32)

    def clear_planes(planes, kind):
        for s in range(2):
            R[s, kind, ROW0 - 2 : ROW0 + BX + 2, :] = zrows
        for f in range(4):
            for z in planes:
                V[f, z, ROW0 - 2 : ROW0 + BX + 2, :] = zrows

    @pl.when(gz == 0)
    def _():
        clear_planes((0, 1), 2)

    @pl.when(gz == nz - 1)
    def _():
        clear_planes((BZ + 2, BZ + 3), 3)

    for s, edge in ((0, 0), (1, ny - 1)):
        @pl.when(gy == edge)
        def _():
            for k in range(4):
                R[s, k, ROW0 - 2 : ROW0 + BX + 2, :] = zrows

    load_m.wait()
    load_t.wait()
    load_o.wait()
    depth_total = BZ * nz
    TB[...] = jnp.zeros(TB.shape, f32)
    for c in range(4):
        entries = jnp.broadcast_to(table[c : c + 1, :], (8, table.shape[1]))
        TB[c, :, 0 : table.shape[1]] = entries * (2.0 / depth_total) if c == 3 else entries

    @pl.loop(0, BZ)
    def _(z):
        tables = [TB[c] for c in range(4)]
        for j in range(4):
            index = M[z, pl.ds(j, 8, stride=4), :]
            for c in range(4):
                LK[z, c, j] = jnp.take_along_axis(tables[c], index, axis=1)

    for n, (dz, dx, dy) in enumerate(OFFSETS):
        @pl.when(there(-dz, -dx, -dy))
        def _():
            for c in copies(n, dz, dx, dy):
                c.wait_recv()

    pl.semaphore_wait(greeted.at[0], 2)
    greet(1)

    on = lambda cond: cond.astype(f32)
    low_x = jnp.where(sub == 0, on(gx > 0), 1.0)
    high_x = jnp.where(sub == 7, on(gx < nx - 1), 1.0)
    low_z, high_z = on(gz > 0), on(gz < nz - 1)
    y_first = jnp.where(lane == 0, on(gy == 0), 0.0)
    y_last = jnp.where(lane == 127, on(gy == ny - 1), 0.0)
    six = 6.0 - y_first - y_last
    edge_sign = y_first - y_last

    def x_mask(cells):
        return [cells[0] * low_x] + cells[1:5] + [cells[5] * high_x]

    def packed(s, k, js):
        return [R[s, k, pl.ds(ROW0 + j, 8, stride=4), :] for j in js]

    js = range(-2, 6)
    near = [packed(0, k, js) for k in range(4)]
    far = [packed(1, k, js) for k in range(4)]
    dens = [
        blur3([jnp.where(lane4 < 2, a, b) for a, b in zip(near[k], far[k])]) for k in (0, 2, 3)
    ]
    for j in range(6):
        u, lo, hi = dens[0][j], dens[1][j], dens[2][j]
        below = jnp.where(lane < 4, lo, pltpu.roll(u, 4, 1))
        above = jnp.where(lane >= 124, hi, pltpu.roll(u, 124, 1))
        mask = low_x if j == 0 else high_x if j == 5 else None
        w = below + 2.0 * u + above
        w_lo = (pltpu.roll(lo, 124, 1) + 2.0 * lo + u) * low_z
        w_hi = (pltpu.roll(hi, 4, 1) + 2.0 * hi + u) * high_z
        if mask is not None:
            w, w_lo, w_hi = w * mask, w_lo * mask, w_hi * mask
        WD[j] = w
        WDE[0, j] = w_lo
        WDE[1, j] = w_hi

    def pair(f, k):
        cells = []
        for a, b in zip(near[k][1:7], far[k][1:7]):
            if f == 1:
                cells.append(jnp.where(lane4 == 2, a, pltpu.roll(b, 3, 1)))
            elif f == 2:
                cells.append(jnp.where(lane4 == 2, pltpu.roll(a, 127, 1), pltpu.roll(b, 2, 1)))
            else:
                cells.append(jnp.where(lane4 == 0, a, b))
        return blur3(cells)

    for f in (1, 2, 3):
        main = pair(f, 1 if f == 3 else 0)
        lo, hi = pair(f, 2), pair(f, 3)
        for j in range(4):
            lo_j, hi_j = lo[j], hi[j]
            if f == 3:
                lo_j, hi_j = pltpu.roll(lo_j, 120, 1), pltpu.roll(hi_j, 8, 1)
            below = jnp.where(lane < 4, lo_j, pltpu.roll(main[j], 4, 1))
            above = jnp.where(lane >= 124, hi_j, pltpu.roll(main[j], 124, 1))
            WF[f - 1, j] = below + 2.0 * main[j] + above

    first, last = lane == 0, lane == 127
    first2, last2 = lane <= 1, lane >= 126

    def x_blur(f, plane, js):
        return blur3([V[f, plane, pl.ds(ROW0 + j, 8, stride=4), :] for j in js])

    def density_plane(z, w, edges):
        by, sy = [], []
        for j in range(6):
            a, e = w[j], edges[j]
            l1 = pltpu.roll(jnp.where(last, e, a), 1, 1)
            l2 = pltpu.roll(jnp.where(last2, e, a), 2, 1)
            r1 = pltpu.roll(jnp.where(first, e, a), 127, 1)
            r2 = pltpu.roll(jnp.where(first2, e, a), 126, 1)
            p1, m1 = l1 + r1, r1 - l1
            by.append((l2 + r2) + 4.0 * p1 + a * six)
            sy.append((r2 - l2) + 2.0 * m1 + a * edge_sign)
            if 1 <= j <= 4:
                D[z + 1, j - 1] = p1 + 2.0 * a
        bb = blur3(by)
        bs = blur3(sy)
        for j in range(4):
            G[0, z + 1, j] = bb[j]
            G[1, z + 1, j] = by[j + 2] - by[j]
            G[2, z + 1, j] = bs[j]

    def blend(a, b, c):
        return [p + 2.0 * q + r for p, q, r in zip(a, b, c)]

    u0 = x_blur(0, 0, js)
    u1 = x_blur(0, 1, js)
    u2 = x_blur(0, 2, js)
    w = x_mask([x * low_z for x in blend(u0, u1, u2)])
    density_plane(-1, w, [pltpu.roll(WDE[0, j], 126, 1) for j in range(6)])

    def density_step(z, carry):
        before, here = carry[:6], carry[6:]
        after = x_blur(0, z + 3, js)
        w = x_mask(blend(before, here, after))
        amount = lax.rem(126 - 4 * z + 128, 128)
        density_plane(z, w, [pltpu.roll(WD[j], amount, 1) for j in range(6)])
        return tuple(here) + tuple(after)

    def density_two(i, carry):
        return density_step(2 * i + 1, density_step(2 * i, carry))

    carry = lax.fori_loop(0, BZ // 2, density_two, tuple(u1) + tuple(u2))
    u3 = x_blur(0, BZ + 3, js)
    w = x_mask([x * high_z for x in blend(carry[:6], carry[6:], u3)])
    density_plane(BZ, w, [pltpu.roll(WDE[1, j], 2, 1) for j in range(6)])

    pl.semaphore_wait(greeted.at[1], 2)
    greet(2)

    js1 = range(-1, 5)

    def field_step(z, carry):
        new = []
        for f in (1, 2, 3):
            before = carry[8 * (f - 1) : 8 * (f - 1) + 4]
            here = carry[8 * (f - 1) + 4 : 8 * f]
            after = x_blur(f, z + 3, js1)
            w = blend(before, here, after)
            amount = lax.rem((127 if f == 3 else 125) - 4 * z + 128, 128)
            for j in range(4):
                e = pltpu.roll(WF[f - 1, j], amount, 1)
                l1 = pltpu.roll(jnp.where(last, e, w[j]), 1, 1)
                r1 = pltpu.roll(jnp.where(first, e, w[j]), 127, 1)
                SM[z, f - 1, j] = l1 + r1 + 2.0 * w[j]
            new += list(here) + list(after)
        return tuple(new)

    def field_two(i, carry):
        return field_step(2 * i + 1, field_step(2 * i, carry))

    carry = []
    for f in (1, 2, 3):
        carry += x_blur(f, 1, js1) + x_blur(f, 2, js1)
    lax.fori_loop(0, BZ // 2, field_two, tuple(carry))

    to_exp2 = 3.0 / (64.0 * math.log(2.0))

    def shade_step(z, carry):
        light, depth, red, green, blue = (list(carry[4 * k : 4 * k + 4]) for k in range(5))
        colour = [red, green, blue]
        for j in range(4):
            g_z = G[0, z + 2, j] - G[0, z, j]
            g_x = G[1, z, j] + 2.0 * G[1, z + 1, j] + G[1, z + 2, j]
            g_y = G[2, z, j] + 2.0 * G[2, z + 1, j] + G[2, z + 2, j]
            facing = jnp.abs(2.0 * (g_z + g_y) + g_x)
            norm = g_z * g_z + g_x * g_x + g_y * g_y + 0.0025 * 2048.0 * 2048.0
            shading = 0.3 + 0.4 * facing * lax.rsqrt(norm)
            grown = jnp.exp2(D[z + 1, j] * to_exp2)
            soft = jnp.where(
                grown < 1.0 / 128.0,
                grown * (1.0 + grown * (-0.5 + grown * (1.0 / 3.0))),
                jnp.log(1.0 + grown),
            )
            e = LK[z, 3, j] * soft
            taken = e * (
                1.0 + e * (-0.5 + e * (1.0 / 6.0 + e * (-1.0 / 24.0 + e * (1.0 / 120.0))))
            )
            weight = light[j] * taken
            light[j] = light[j] - weight
            depth[j] = depth[j] + e
            lit = weight * shading
            for c in range(3):
                tone = 1.0 + 0.5 * jnp.tanh(SM[z, c, j] * (1.0 / 64.0))
                colour[c][j] = colour[c][j] + lit * (LK[z, c, j] * tone)
        return tuple(light + depth + colour[0] + colour[1] + colour[2])

    def shade_two(i, carry):
        return shade_step(2 * i + 1, shade_step(2 * i, carry))

    zero = jnp.zeros((8, 128), f32)
    final = lax.fori_loop(
        0, BZ // 2, shade_two, tuple([jnp.ones((8, 128), f32)] * 4 + [zero] * 16)
    )

    pl.semaphore_wait(greeted.at[2], 2)

    for c, k in ((0, 2), (1, 3), (2, 4), (3, 1)):
        for j in range(4):
            SB[pl.ds(8 * (j // 2) + 2 * c + j % 2, 8, stride=16), :] = final[4 * k + j]

    def to_peer(k):
        peer = lax.rem(gz + k, nz)
        return pltpu.make_async_remote_copy(
            src_ref=SB.at[pl.ds(pl.multiple_of(peer * 8, 8), 8)],
            dst_ref=RB.at[pl.ds(pl.multiple_of(gz * 8, 8), 8)],
            send_sem=a2a_send.at[k],
            recv_sem=a2a_recv.at[k],
            device_id={"gz": peer},
            device_id_type=MESH,
        )

    far_first = sorted(range(1, nz), key=lambda k: (-min(k, nz - k), k))
    for k in far_first:
        to_peer(k).start()
    own = pl.ds(pl.multiple_of(gz * 8, 8), 8)
    RB[own, :] = SB[own, :]
    for n, (dz, dx, dy) in enumerate(OFFSETS):
        @pl.when(there(dz, dx, dy))
        def _():
            for c in copies(n, dz, dx, dy):
                c.wait_send()
    for k in reversed(far_first):
        to_peer(k).wait_recv()

    parts = [RB[8 * b : 8 * b + 8, :] for b in range(nz)]
    depths = []
    for part in parts:
        d = jnp.where(sub >= 6, part, 0.0)
        d = d + pltpu.roll(d, 4, 0)
        depths.append(d + pltpu.roll(d, 2, 0))
    total = depths[0]
    for d in depths[1:]:
        total = total + d
    image = zero
    for b in range(nz):
        prior = zero
        for o in range(nz):
            if o != b:
                prior = prior + jnp.where(order[o] < order[b], depths[o], 0.0)
        image = image + jnp.exp(-prior) * parts[b]
    small = total * (
        1.0 + total * (-0.5 + total * (1.0 / 6.0 + total * (-1.0 / 24.0 + total * (1.0 / 120.0))))
    )
    opacity = jnp.where(total < 0.125, small, 1.0 - jnp.exp(-total))
    image = jnp.where(sub >= 6, opacity, image)
    for c in range(4):
        out[c] = image[2 * c : 2 * c + 2, :]
    for k in far_first:
        to_peer(k).wait_send()


def on_device(fields, material, depth_order, table):
    vmem = lambda *shape: pltpu.VMEM(shape, f32)
    dma = pltpu.SemaphoreType.DMA
    count = len(OFFSETS)
    return pl.pallas_call(
        kernel,
        out_shape=pltpu.VMEM((4, 2, 128), f32),
        in_specs=[pl.BlockSpec(memory_space=pl.ANY)] * 4,
        out_specs=pl.BlockSpec(memory_space=pltpu.VMEM),
        scratch_shapes=[
            vmem(4, BZ + 4, ROWS, 128),
            pltpu.VMEM((BZ, BX, 128), jnp.int32),
            vmem(2, 4, BX, 128),
            vmem(2, 4, ROWS, 128),
            vmem(6, 8, 128),
            vmem(2, 6, 8, 128),
            vmem(3, 4, 8, 128),
            vmem(3, BZ + 2, 4, 8, 128),
            vmem(BZ + 2, 4, 8, 128),
            vmem(BZ, 3, 4, 8, 128),
            vmem(BZ, 4, 4, 8, 128),
            vmem(4, 8, 128),
            vmem(4, 16),
            pltpu.SMEM((16,), jnp.int32),
            vmem(128, 128),
            vmem(128, 128),
            dma((7,)),
            dma((count, 2)),
            dma((count, 2)),
            dma((16,)),
            dma((16,)),
            pltpu.SemaphoreType.REGULAR((3,)),
        ],
        compiler_params=pltpu.CompilerParams(collective_id=0, has_side_effects=True),
    )(fields, material, depth_order, table)


def solution(mesh):
    return jax.shard_map(
        on_device,
        mesh=mesh,
        in_specs=(P(None, "gz", "gx", "gy"), P("gz", "gx", "gy"), P(), P()),
        out_specs=P(None, ("gx", "gz"), "gy"),
        check_vma=False,
    )
```

```python
import math

import jax
import jax.numpy as jnp
from jax import lax
from jax.experimental import pallas as pl
from jax.experimental.pallas import tpu as pltpu
from jax.sharding import PartitionSpec as P

MESH = pl.DeviceIdType.MESH
f32 = jnp.float32
bf16 = jnp.bfloat16

BZ = 32
BX = 32
ROW0 = 8
ROWS = 48

OFFSETS = [
    (dz, dx, dy)
    for dz in (-1, 0, 1)
    for dx in (-1, 0, 1)
    for dy in (-1, 0, 1)
    if (dz, dx, dy) != (0, 0, 0)
]
OFFSETS.sort(key=lambda o: -abs(o[0]) - abs(o[1]) - abs(o[2]))


def z_range(dz, width):
    if dz == 1:
        return pl.ds(BZ - width, width), pl.ds(2 - width, width)
    if dz == -1:
        return pl.ds(0, width), pl.ds(2 + BZ, width)
    return pl.ds(0, BZ), pl.ds(2, BZ)


def x_range(dx, width):
    if dx == 1:
        return pl.ds(BX - width, width), pl.ds(ROW0 - width, width)
    if dx == -1:
        return pl.ds(0, width), pl.ds(ROW0 + BX, width)
    return pl.ds(0, BX), pl.ds(ROW0, BX)


def blur3(cells):
    pairs = [a + b for a, b in zip(cells[:-1], cells[1:])]
    return [a + b for a, b in zip(pairs[:-1], pairs[1:])]


def split(a):
    high = a.astype(bf16)
    rest = a - high.astype(f32)
    middle = rest.astype(bf16)
    return high, middle, (rest - middle.astype(f32)).astype(bf16)


def blur_weight(d):
    return jnp.where(d == 0, 2.0, jnp.where(jnp.abs(d) == 1, 1.0, 0.0))


def blur2_weight(d):
    far = jnp.abs(d)
    return jnp.where(
        far == 0, 6.0, jnp.where(far == 1, 4.0, jnp.where(far == 2, 1.0, 0.0))
    )


def slope_weight(d):
    far = jnp.abs(d)
    size = jnp.where(far == 1, 2.0, jnp.where(far == 2, 1.0, 0.0))
    return jnp.where(d > 0, size, -size)


def kernel(
    fields, material, order_hbm, table_hbm, out,
    V, M, S, R, PE, H, TD, TF, DD, SM, LK, TB, table, order, at_rank, SB, RB,
    load_sem, send_sem, recv_sem, a2a_send, a2a_recv, greeted,
):
    gz, gx, gy = lax.axis_index("gz"), lax.axis_index("gx"), lax.axis_index("gy")
    nz, nx, ny = lax.axis_size("gz"), lax.axis_size("gx"), lax.axis_size("gy")

    def there(dz, dx, dy):
        ok = None
        for pos, d, n in ((gz, dz, nz), (gx, dx, nx), (gy, dy, ny)):
            if d == 0:
                continue
            this = pos < n - 1 if d == 1 else pos > 0
            ok = this if ok is None else jnp.logical_and(ok, this)
        return ok

    loads = [
        pltpu.make_async_copy(
            fields.at[f], V.at[f, pl.ds(2, BZ), pl.ds(ROW0, BX)], load_sem.at[f]
        )
        for f in range(4)
    ]
    load_m = pltpu.make_async_copy(material, M, load_sem.at[4])
    load_t = pltpu.make_async_copy(table_hbm, table, load_sem.at[5])
    load_o = pltpu.make_async_copy(order_hbm, order, load_sem.at[6])
    for c in loads:
        c.start()
    load_m.start()
    load_t.start()
    load_o.start()

    barrier = pltpu.get_barrier_semaphore()
    for dz, dx, dy in OFFSETS:
        @pl.when(there(dz, dx, dy))
        def _():
            pl.semaphore_signal(
                barrier,
                inc=1,
                device_id={"gz": gz + dz, "gx": gx + dx, "gy": gy + dy},
                device_id_type=MESH,
            )

    def greet(k):
        for to in (gz + (1 << k), gz - (1 << k)):
            @pl.when(jnp.logical_and(to >= 0, to < nz))
            def _():
                pl.semaphore_signal(
                    greeted.at[k], inc=1, device_id={"gz": to}, device_id_type=MESH
                )

    def await_greetings(k):
        count = (gz >= 1 << k).astype(jnp.int32) + (gz + (1 << k) < nz).astype(jnp.int32)
        pl.semaphore_wait(greeted.at[k], count)

    def span(pos, n):
        return 1 + (pos > 0).astype(jnp.int32) + (pos < n - 1).astype(jnp.int32)

    expected = span(gz, nz) * span(gx, nx) * span(gy, ny) - 1

    lane = lax.broadcasted_iota(jnp.int32, (8, 128), 1)
    sub = lax.broadcasted_iota(jnp.int32, (8, 128), 0)
    lane4 = lane % 4
    lane_z = lane // 4

    acc = [[jnp.zeros((8, 128), f32)] * 4 for _ in range(4)]
    shift0 = (2, 3, 3, 1)
    for f in range(4):
        loads[f].wait()
        for z in range(BZ):
            mask = lane_z == z
            for i in range(4):
                tile = V[f, z + 2, ROW0 + 8 * i : ROW0 + 8 * i + 8, :]
                moved = pltpu.roll(tile, (4 * z + shift0[f]) % 128, 1)
                acc[f][i] = jnp.where(mask, moved, acc[f][i])
    for i in range(4):
        ad, a1, a2, b = (acc[f][i] for f in range(4))
        front = jnp.where(lane4 < 2, ad, jnp.where(lane4 == 2, a1, pltpu.roll(a2, 1, 1)))
        back = jnp.where(
            lane4 >= 2, ad, jnp.where(lane4 == 0, pltpu.roll(a1, 125, 1), pltpu.roll(a2, 126, 1))
        )
        for s, a in ((0, front), (1, back)):
            rows = pl.ds(8 * i, 8)
            S[s, 0, rows, :] = a
            S[s, 1, rows, :] = b
            S[s, 2, rows, :] = jnp.where(
                lane < 4,
                pltpu.roll(a, 4, 1),
                jnp.where(lane < 8, pltpu.roll(a, 12, 1), pltpu.roll(b, 12, 1)),
            )
            S[s, 3, rows, :] = jnp.where(
                lane >= 124,
                pltpu.roll(a, 124, 1),
                jnp.where(lane >= 120, pltpu.roll(a, 116, 1), pltpu.roll(b, 116, 1)),
            )

    def copies(n, dz, dx, dy):
        device = {"gz": gz + dz, "gx": gx + dx, "gy": gy + dy}

        def make(src, dst, k):
            return pltpu.make_async_remote_copy(
                src_ref=src,
                dst_ref=dst,
                send_sem=send_sem.at[n, k],
                recv_sem=recv_sem.at[n, k],
                device_id=device,
                device_id_type=MESH,
            )

        xs2, xd2 = x_range(dx, 2)
        if dy == 0:
            zs2, zd2 = z_range(dz, 2)
            zs1, zd1 = z_range(dz, 1)
            xs1, xd1 = x_range(dx, 1)
            return [
                make(fields.at[0, zs2, xs2], V.at[0, zd2, xd2], 0),
                make(fields.at[pl.ds(1, 3), zs1, xs1], V.at[pl.ds(1, 3), zd1, xd1], 1),
            ]
        side = 0 if dy == 1 else 1
        kinds = {0: pl.ds(0, 2), 1: pl.ds(2, 1), -1: pl.ds(3, 1)}[dz]
        return [make(S.at[side, kinds, xs2], R.at[side, kinds, xd2], 0)]

    pl.semaphore_wait(barrier, expected)
    for n, (dz, dx, dy) in enumerate(OFFSETS):
        @pl.when(there(dz, dx, dy))
        def _():
            for c in copies(n, dz, dx, dy):
                c.start()

    greet(0)

    zrow = jnp.zeros((2, 128), f32)

    @pl.when(gx == 0)
    def _():
        for s in range(2):
            for k in range(4):
                R[s, k, ROW0 - 2 : ROW0, :] = zrow

        @pl.loop(0, BZ + 4)
        def _(z):
            for f in range(4):
                V[f, z, ROW0 - 2 : ROW0, :] = zrow

    @pl.when(gx == nx - 1)
    def _():
        for s in range(2):
            for k in range(4):
                R[s, k, ROW0 + BX : ROW0 + BX + 2, :] = zrow

        @pl.loop(0, BZ + 4)
        def _(z):
            for f in range(4):
                V[f, z, ROW0 + BX : ROW0 + BX + 2, :] = zrow

    zrows = jnp.zeros((BX + 4, 128), f32)

    def clear_planes(planes, kind):
        for s in range(2):
            R[s, kind, ROW0 - 2 : ROW0 + BX + 2, :] = zrows
        for f in range(4):
            for z in planes:
                V[f, z, ROW0 - 2 : ROW0 + BX + 2, :] = zrows

    @pl.when(gz == 0)
    def _():
        clear_planes((0, 1), 2)

    @pl.when(gz == nz - 1)
    def _():
        clear_planes((BZ + 2, BZ + 3), 3)

    for s, edge in ((0, 0), (1, ny - 1)):
        @pl.when(gy == edge)
        def _():
            for k in range(4):
                R[s, k, ROW0 - 2 : ROW0 + BX + 2, :] = zrows

    await_greetings(0)
    greet(1)

    load_m.wait()
    load_t.wait()
    load_o.wait()
    for rank in range(nz):
        layer = 0
        for o in range(nz):
            layer = jnp.where(order[o] == rank, o, layer)
        at_rank[rank] = layer
    depth_total = BZ * nz
    for c in range(4):
        for m in range(16):
            entry = table[c, m] * (2.0 / depth_total) if c == 3 else table[c, m]
            TB[16 * c + m] = jnp.broadcast_to(entry, (8, 128))

    row = lax.broadcasted_iota(jnp.int32, (128, 128), 0)
    col = lax.broadcasted_iota(jnp.int32, (128, 128), 1)
    row4 = row % 4
    beside = jnp.where(row4 < 2, row4 - 2, row4 + 126)
    beside1 = jnp.where(row4 == 2, -1, jnp.where(row4 == 3, 128, -1000))
    first_y = jnp.where((row == 0) & (col == 0), (gy == 0).astype(f32), 0.0)
    last_y = jnp.where((row == 127) & (col == 127), (gy == ny - 1).astype(f32), 0.0)
    own = jnp.concatenate(
        [
            blur_weight(row - col),
            blur2_weight(row - col) - first_y - last_y,
            slope_weight(row - col) + first_y - last_y,
        ],
        axis=1,
    ).astype(bf16)
    for k in range(3):
        TD[128 * k : 128 * k + 128, :] = own
        TF[128 * k : 128 * k + 128, :] = own[:, 0:128]
    TD[384:512, :] = jnp.concatenate(
        [weight(beside - col) for weight in (blur_weight, blur2_weight, slope_weight)], axis=1
    ).astype(bf16)
    TF[384:512, :] = blur_weight(beside1 - col).astype(bf16)

    @pl.loop(0, BZ)
    def _(z):
        bits = []
        for j in range(4):
            index = M[z, pl.ds(j, 8, stride=4), :]
            bits.append([(index & (1 << k)) != 0 for k in range(4)])
        for c in range(4):
            entries = [TB[16 * c + m] for m in range(16)]
            for j in range(4):
                left = entries
                for k in range(4):
                    left = [jnp.where(bits[j][k], b, a) for a, b in zip(left[::2], left[1::2])]
                LK[z, c, j] = left[0]

    await_greetings(1)
    greet(2)

    for n, (dz, dx, dy) in enumerate(OFFSETS):
        @pl.when(there(-dz, -dx, -dy))
        def _():
            for c in copies(n, dz, dx, dy):
                c.wait_recv()

    await_greetings(2)
    greet(3)

    on = lambda cond: cond.astype(f32)
    low_x = jnp.where(sub == 0, on(gx > 0), 1.0)
    high_x = jnp.where(sub == 7, on(gx < nx - 1), 1.0)
    low_z, high_z = on(gz > 0), on(gz < nz - 1)
    def x_mask(cells):
        return [cells[0] * low_x] + cells[1:5] + [cells[5] * high_x]

    def packed(s, k, js):
        return [R[s, k, pl.ds(ROW0 + j, 8, stride=4), :] for j in js]

    js = range(-2, 6)
    near = [packed(0, k, js) for k in range(4)]
    far = [packed(1, k, js) for k in range(4)]
    dens = [
        blur3([jnp.where(lane4 < 2, a, b) for a, b in zip(near[k], far[k])]) for k in (0, 2, 3)
    ]
    packed_main, packed_low, packed_high = [], [], []
    for j in range(6):
        u, lo, hi = dens[0][j], dens[1][j], dens[2][j]
        below = jnp.where(lane < 4, lo, pltpu.roll(u, 4, 1))
        above = jnp.where(lane >= 124, hi, pltpu.roll(u, 124, 1))
        mask = low_x if j == 0 else high_x if j == 5 else None
        w = below + 2.0 * u + above
        w_lo = (pltpu.roll(lo, 124, 1) + 2.0 * lo + u) * low_z
        w_hi = (pltpu.roll(hi, 4, 1) + 2.0 * hi + u) * high_z
        if mask is not None:
            w, w_lo, w_hi = w * mask, w_lo * mask, w_hi * mask
        packed_main.append(w)
        packed_low.append(w_lo)
        packed_high.append(w_hi)

    def keep(slot, cells):
        for p in range(len(cells) // 2):
            parts = split(jnp.concatenate([cells[2 * p], cells[2 * p + 1]], axis=0))
            for k in range(3):
                part = parts[k].astype(f32)
                PE[slot, p, k] = pltpu.roll(part, 44 * k, 1) if k else part

    keep(0, packed_main)
    keep(1, packed_low)
    keep(2, packed_high)

    def pair(f, k):
        cells = []
        for a, b in zip(near[k][1:7], far[k][1:7]):
            if f == 1:
                cells.append(jnp.where(lane4 == 2, a, pltpu.roll(b, 3, 1)))
            elif f == 2:
                cells.append(jnp.where(lane4 == 2, pltpu.roll(a, 127, 1), pltpu.roll(b, 2, 1)))
            else:
                cells.append(pltpu.roll(jnp.where(lane4 == 0, a, b), 2, 1))
        return blur3(cells)

    for f in (1, 2, 3):
        main = pair(f, 1 if f == 3 else 0)
        lo, hi = pair(f, 2), pair(f, 3)
        cells = []
        for j in range(4):
            lo_j, hi_j = lo[j], hi[j]
            if f == 3:
                lo_j, hi_j = pltpu.roll(lo_j, 120, 1), pltpu.roll(hi_j, 8, 1)
            below = jnp.where(lane < 4, lo_j, pltpu.roll(main[j], 4, 1))
            above = jnp.where(lane >= 124, hi_j, pltpu.roll(main[j], 124, 1))
            cells.append(below + 2.0 * main[j] + above)
        keep(2 + f, cells)

    def x_blur(f, plane, js):
        return blur3([V[f, plane, pl.ds(ROW0 + j, 8, stride=4), :] for j in js])

    def blend(a, b, c):
        return [p + 2.0 * q + r for p, q, r in zip(a, b, c)]

    group = lax.broadcasted_iota(jnp.int32, (16, 128), 1) // 4

    def put(base, slot, cells, z):
        masks = [group == lax.rem(z + 11 * k, BZ) for k in range(3)]
        for p in range(len(cells) // 2):
            rows = pl.ds(pl.multiple_of(base + 16 * p, 16), 16)
            parts = split(jnp.concatenate([cells[2 * p], cells[2 * p + 1]], axis=0))
            for k in range(3):
                H[rows, 128 * k : 128 * k + 128] = parts[k]
            beside = jnp.where(masks[2], PE[slot, p, 2], 0.0)
            beside = jnp.where(masks[1], PE[slot, p, 1], beside)
            beside = jnp.where(masks[0], PE[slot, p, 0], beside)
            H[rows, 384:512] = beside.astype(bf16)

    u0 = x_blur(0, 0, js)
    u1 = x_blur(0, 1, js)
    u2 = x_blur(0, 2, js)
    put(0, 1, x_mask([x * low_z for x in blend(u0, u1, u2)]), 0)

    def density_step(z, carry):
        before, here = carry[:6], carry[6:]
        after = x_blur(0, z + 3, js)
        put(48 * z + 48, 0, x_mask(blend(before, here, after)), z)
        return tuple(here) + tuple(after)

    def density_two(i, carry):
        return density_step(2 * i + 1, density_step(2 * i, carry))

    carry = lax.fori_loop(0, BZ // 2, density_two, tuple(u1) + tuple(u2))
    u3 = x_blur(0, BZ + 3, js)
    put(48 * BZ + 48, 2, x_mask([x * high_z for x in blend(carry[:6], carry[6:], u3)]), BZ - 1)
    for k in range(2):
        rows = pl.ds(816 * k, 816)
        DD[rows, :] = jnp.dot(H[rows, :], TD[...], preferred_element_type=f32)

    js1 = range(-1, 5)

    def field_step(z, carry):
        new = []
        for f in (1, 2, 3):
            before = carry[8 * (f - 1) : 8 * (f - 1) + 4]
            here = carry[8 * (f - 1) + 4 : 8 * f]
            after = x_blur(f, z + 3, js1)
            put(96 * z + 32 * (f - 1), 2 + f, blend(before, here, after), z)
            new += list(here) + list(after)
        return tuple(new)

    def field_two(i, carry):
        return field_step(2 * i + 1, field_step(2 * i, carry))

    carry = []
    for f in (1, 2, 3):
        carry += x_blur(f, 1, js1) + x_blur(f, 2, js1)
    lax.fori_loop(0, BZ // 2, field_two, tuple(carry))
    for k in range(4):
        rows = pl.ds(768 * k, 768)
        SM[rows, :] = jnp.dot(H[rows, :], TF[...], preferred_element_type=f32)

    to_exp2 = 3.0 / (64.0 * math.log(2.0))

    def shade_step(z, carry):
        light, depth, red, green, blue = (list(carry[4 * k : 4 * k + 4]) for k in range(5))
        colour = [red, green, blue]

        def part(plane, j, c):
            return DD[pl.ds(pl.multiple_of(48 * (z + plane) + 8 * j, 8), 8), 128 * c : 128 * c + 128]

        by = [[part(p, j, 1) for j in range(6)] for p in range(3)]
        sy = [[part(p, j, 2) for j in range(6)] for p in range(3)]
        along_z = blur3([b - a for a, b in zip(by[0], by[2])])
        across = blend(*by)
        along_y = blur3(blend(*sy))
        for j in range(4):
            g_z, g_x, g_y = along_z[j], across[j + 2] - across[j], along_y[j]
            facing = jnp.abs(2.0 * (g_z + g_y) + g_x)
            norm = g_z * g_z + g_x * g_x + g_y * g_y + 0.0025 * 2048.0 * 2048.0
            shading = 0.3 + 0.4 * facing * lax.rsqrt(norm)
            grown = jnp.exp2(part(1, j + 1, 0) * to_exp2)
            soft = jnp.where(
                grown < 1.0 / 128.0,
                grown * (1.0 + grown * (-0.5 + grown * (1.0 / 3.0))),
                jnp.log(1.0 + grown),
            )
            e = LK[z, 3, j] * soft
            taken = e * (
                1.0 + e * (-0.5 + e * (1.0 / 6.0 + e * (-1.0 / 24.0 + e * (1.0 / 120.0))))
            )
            weight = light[j] * taken
            light[j] = light[j] - weight
            depth[j] = depth[j] + e
            lit = weight * shading
            for c in range(3):
                smooth = SM[pl.ds(pl.multiple_of(96 * z + 32 * c + 8 * j, 8), 8), :]
                tone = 1.0 + 0.5 * jnp.tanh(smooth * (1.0 / 64.0))
                colour[c][j] = colour[c][j] + lit * (LK[z, c, j] * tone)
        return tuple(light + depth + colour[0] + colour[1] + colour[2])

    def shade_two(i, carry):
        return shade_step(2 * i + 1, shade_step(2 * i, carry))

    zero = jnp.zeros((8, 128), f32)
    final = lax.fori_loop(
        0, BZ // 2, shade_two, tuple([jnp.ones((8, 128), f32)] * 4 + [zero] * 16)
    )

    await_greetings(3)

    for c, k in ((0, 2), (1, 3), (2, 4), (3, 1)):
        for j in range(4):
            SB[pl.ds(8 * (j // 2) + 2 * c + j % 2, 8, stride=16), :] = final[4 * k + j]

    def to_peer(k):
        peer = lax.rem(gz + k, nz)
        return pltpu.make_async_remote_copy(
            src_ref=SB.at[pl.ds(pl.multiple_of(peer * 8, 8), 8)],
            dst_ref=RB.at[gz],
            send_sem=a2a_send.at[k],
            recv_sem=a2a_recv.at[k],
            device_id={"gz": peer},
            device_id_type=MESH,
        )

    far_first = sorted(range(1, nz), key=lambda k: (-min(k, nz - k), k))
    for k in far_first:
        to_peer(k).start()
    own = pl.ds(pl.multiple_of(gz * 8, 8), 8)
    RB[gz] = SB[own, :]
    for n, (dz, dx, dy) in enumerate(OFFSETS):
        @pl.when(there(dz, dx, dy))
        def _():
            for c in copies(n, dz, dx, dy):
                c.wait_send()
    for k in far_first:
        to_peer(k).wait_send()
    for k in reversed(far_first):
        to_peer(k).wait_recv()

    total, image = zero, zero
    for rank in range(nz):
        part = RB[at_rank[rank]]
        image = image + jnp.exp(-total) * part
        d = jnp.where(sub >= 6, part, 0.0)
        d = d + pltpu.roll(d, 4, 0)
        total = total + (d + pltpu.roll(d, 2, 0))
    small = total * (
        1.0 + total * (-0.5 + total * (1.0 / 6.0 + total * (-1.0 / 24.0 + total * (1.0 / 120.0))))
    )
    opacity = jnp.where(total < 0.125, small, 1.0 - jnp.exp(-total))
    image = jnp.where(sub >= 6, opacity, image)
    for c in range(4):
        out[c] = image[2 * c : 2 * c + 2, :]


def on_device(fields, material, depth_order, table):
    vmem = lambda *shape: pltpu.VMEM(shape, f32)
    dma = pltpu.SemaphoreType.DMA
    count = len(OFFSETS)
    return pl.pallas_call(
        kernel,
        out_shape=pltpu.VMEM((4, 2, 128), f32),
        in_specs=[pl.BlockSpec(memory_space=pl.ANY)] * 4,
        out_specs=pl.BlockSpec(memory_space=pltpu.VMEM),
        scratch_shapes=[
            vmem(4, BZ + 4, ROWS, 128),
            pltpu.VMEM((BZ, BX, 128), jnp.int32),
            vmem(2, 4, BX, 128),
            vmem(2, 4, ROWS, 128),
            vmem(6, 3, 3, 16, 128),
            pltpu.VMEM((96 * BZ, 512), bf16),
            pltpu.VMEM((512, 384), bf16),
            pltpu.VMEM((512, 128), bf16),
            vmem(48 * (BZ + 2), 384),
            vmem(96 * BZ, 128),
            vmem(BZ, 4, 4, 8, 128),
            vmem(64, 8, 128),
            pltpu.SMEM((4, 16), f32),
            pltpu.SMEM((16,), jnp.int32),
            pltpu.SMEM((16,), jnp.int32),
            vmem(128, 128),
            vmem(16, 8, 128),
            dma((7,)),
            dma((count, 2)),
            dma((count, 2)),
            dma((16,)),
            dma((16,)),
            pltpu.SemaphoreType.REGULAR((4,)),
        ],
        compiler_params=pltpu.CompilerParams(collective_id=0, has_side_effects=True),
    )(fields, material, depth_order, table)


def solution(mesh):
    return jax.shard_map(
        on_device,
        mesh=mesh,
        in_specs=(P(None, "gz", "gx", "gy"), P("gz", "gx", "gy"), P(), P()),
        out_specs=P(None, ("gx", "gz"), "gy"),
        check_vma=False,
    )
```

```python
import math

import jax
import jax.numpy as jnp
from jax import lax
from jax.experimental import pallas as pl
from jax.experimental.pallas import tpu as pltpu
from jax.sharding import PartitionSpec as P

MESH = pl.DeviceIdType.MESH
f32 = jnp.float32
bf16 = jnp.bfloat16

BZ = 32
BX = 32
ROW0 = 8
ROWS = 48

OFFSETS = [
    (dz, dx, dy)
    for dz in (-1, 0, 1)
    for dx in (-1, 0, 1)
    for dy in (-1, 0, 1)
    if (dz, dx, dy) != (0, 0, 0)
]
OFFSETS.sort(key=lambda o: (o[2] == 0, -abs(o[0]) - abs(o[1]) - abs(o[2])))


def z_range(dz, width):
    if dz == 1:
        return pl.ds(BZ - width, width), pl.ds(2 - width, width)
    if dz == -1:
        return pl.ds(0, width), pl.ds(2 + BZ, width)
    return pl.ds(0, BZ), pl.ds(2, BZ)


def x_range(dx, width):
    if dx == 1:
        return pl.ds(BX - width, width), pl.ds(ROW0 - width, width)
    if dx == -1:
        return pl.ds(0, width), pl.ds(ROW0 + BX, width)
    return pl.ds(0, BX), pl.ds(ROW0, BX)


def blur3(cells):
    pairs = [a + b for a, b in zip(cells[:-1], cells[1:])]
    return [a + b for a, b in zip(pairs[:-1], pairs[1:])]


def split(a):
    high = a.astype(bf16)
    rest = a - high.astype(f32)
    middle = rest.astype(bf16)
    return high, middle, (rest - middle.astype(f32)).astype(bf16)


def blur_weight(d):
    return jnp.where(d == 0, 2.0, jnp.where(jnp.abs(d) == 1, 1.0, 0.0))


def blur2_weight(d):
    far = jnp.abs(d)
    return jnp.where(
        far == 0, 6.0, jnp.where(far == 1, 4.0, jnp.where(far == 2, 1.0, 0.0))
    )


def slope_weight(d):
    far = jnp.abs(d)
    size = jnp.where(far == 1, 2.0, jnp.where(far == 2, 1.0, 0.0))
    return jnp.where(d > 0, size, -size)


def kernel(
    fields, material, order_hbm, table_hbm, out,
    V, M, S, R, PE, HD, HF, TD, TF, DD, SM, LK, TB, table, order, at_rank, SB, RB,
    load_sem, send_sem, recv_sem, a2a_send, a2a_recv, greeted,
):
    gz, gx, gy = lax.axis_index("gz"), lax.axis_index("gx"), lax.axis_index("gy")
    nz, nx, ny = lax.axis_size("gz"), lax.axis_size("gx"), lax.axis_size("gy")

    def there(dz, dx, dy):
        ok = None
        for pos, d, n in ((gz, dz, nz), (gx, dx, nx), (gy, dy, ny)):
            if d == 0:
                continue
            this = pos < n - 1 if d == 1 else pos > 0
            ok = this if ok is None else jnp.logical_and(ok, this)
        return ok

    loads = [
        pltpu.make_async_copy(
            fields.at[f], V.at[f, pl.ds(2, BZ), pl.ds(ROW0, BX)], load_sem.at[f]
        )
        for f in range(4)
    ]
    load_m = pltpu.make_async_copy(material, M, load_sem.at[4])
    load_t = pltpu.make_async_copy(table_hbm, table, load_sem.at[5])
    load_o = pltpu.make_async_copy(order_hbm, order, load_sem.at[6])
    loads[0].start()

    barrier = pltpu.get_barrier_semaphore()
    for dz, dx, dy in OFFSETS:
        @pl.when(there(dz, dx, dy))
        def _():
            pl.semaphore_signal(
                barrier,
                inc=1,
                device_id={"gz": gz + dz, "gx": gx + dx, "gy": gy + dy},
                device_id_type=MESH,
            )

    for c in loads[1:]:
        c.start()
    load_m.start()
    load_t.start()
    load_o.start()

    def greet(k):
        for to in (gz + (1 << k), gz - (1 << k)):
            @pl.when(jnp.logical_and(to >= 0, to < nz))
            def _():
                pl.semaphore_signal(
                    greeted.at[k], inc=1, device_id={"gz": to}, device_id_type=MESH
                )

    def await_greetings(k):
        count = (gz >= 1 << k).astype(jnp.int32) + (gz + (1 << k) < nz).astype(jnp.int32)
        pl.semaphore_wait(greeted.at[k], count)

    def span(pos, n):
        return 1 + (pos > 0).astype(jnp.int32) + (pos < n - 1).astype(jnp.int32)

    expected = span(gz, nz) * span(gx, nx) * span(gy, ny) - 1

    lane = lax.broadcasted_iota(jnp.int32, (8, 128), 1)
    sub = lax.broadcasted_iota(jnp.int32, (8, 128), 0)
    lane4 = lane % 4
    lane_z = lane // 4

    acc = [[jnp.zeros((8, 128), f32)] * 4 for _ in range(4)]
    shift0 = (2, 3, 3, 1)
    for f in range(4):
        loads[f].wait()
        for z in range(BZ):
            mask = lane_z == z
            for i in range(4):
                tile = V[f, z + 2, ROW0 + 8 * i : ROW0 + 8 * i + 8, :]
                moved = pltpu.roll(tile, (4 * z + shift0[f]) % 128, 1)
                acc[f][i] = jnp.where(mask, moved, acc[f][i])
    for i in range(4):
        ad, a1, a2, b = (acc[f][i] for f in range(4))
        front = jnp.where(lane4 < 2, ad, jnp.where(lane4 == 2, a1, pltpu.roll(a2, 1, 1)))
        back = jnp.where(
            lane4 >= 2, ad, jnp.where(lane4 == 0, pltpu.roll(a1, 125, 1), pltpu.roll(a2, 126, 1))
        )
        for s, a in ((0, front), (1, back)):
            rows = pl.ds(8 * i, 8)
            S[s, 0, rows, :] = a
            S[s, 1, rows, :] = b
            S[s, 2, rows, :] = jnp.where(
                lane < 4,
                pltpu.roll(a, 4, 1),
                jnp.where(lane < 8, pltpu.roll(a, 12, 1), pltpu.roll(b, 12, 1)),
            )
            S[s, 3, rows, :] = jnp.where(
                lane >= 124,
                pltpu.roll(a, 124, 1),
                jnp.where(lane >= 120, pltpu.roll(a, 116, 1), pltpu.roll(b, 116, 1)),
            )

    def copies(n, dz, dx, dy):
        device = {"gz": gz + dz, "gx": gx + dx, "gy": gy + dy}

        def make(src, dst, k):
            return pltpu.make_async_remote_copy(
                src_ref=src,
                dst_ref=dst,
                send_sem=send_sem.at[n, k],
                recv_sem=recv_sem.at[n, k],
                device_id=device,
                device_id_type=MESH,
            )

        xs2, xd2 = x_range(dx, 2)
        if dy == 0:
            zs2, zd2 = z_range(dz, 2)
            zs1, zd1 = z_range(dz, 1)
            xs1, xd1 = x_range(dx, 1)
            return [
                make(fields.at[0, zs2, xs2], V.at[0, zd2, xd2], 0),
                make(fields.at[pl.ds(1, 3), zs1, xs1], V.at[pl.ds(1, 3), zd1, xd1], 1),
            ]
        side = 0 if dy == 1 else 1
        kinds = {0: pl.ds(0, 2), 1: pl.ds(2, 1), -1: pl.ds(3, 1)}[dz]
        return [make(S.at[side, kinds, xs2], R.at[side, kinds, xd2], 0)]

    pl.semaphore_wait(barrier, expected)
    for n, (dz, dx, dy) in enumerate(OFFSETS):
        @pl.when(there(dz, dx, dy))
        def _():
            for c in copies(n, dz, dx, dy):
                c.start()

    greet(0)

    zrow = jnp.zeros((2, 128), f32)

    @pl.when(gx == 0)
    def _():
        for s in range(2):
            for k in range(4):
                R[s, k, ROW0 - 2 : ROW0, :] = zrow

        @pl.loop(0, BZ + 4)
        def _(z):
            for f in range(4):
                V[f, z, ROW0 - 2 : ROW0, :] = zrow

    @pl.when(gx == nx - 1)
    def _():
        for s in range(2):
            for k in range(4):
                R[s, k, ROW0 + BX : ROW0 + BX + 2, :] = zrow

        @pl.loop(0, BZ + 4)
        def _(z):
            for f in range(4):
                V[f, z, ROW0 + BX : ROW0 + BX + 2, :] = zrow

    zrows = jnp.zeros((BX + 4, 128), f32)

    def clear_planes(planes, kind):
        for s in range(2):
            R[s, kind, ROW0 - 2 : ROW0 + BX + 2, :] = zrows
        for f in range(4):
            for z in planes:
                V[f, z, ROW0 - 2 : ROW0 + BX + 2, :] = zrows

    @pl.when(gz == 0)
    def _():
        clear_planes((0, 1), 2)

    @pl.when(gz == nz - 1)
    def _():
        clear_planes((BZ + 2, BZ + 3), 3)

    for s, edge in ((0, 0), (1, ny - 1)):
        @pl.when(gy == edge)
        def _():
            for k in range(4):
                R[s, k, ROW0 - 2 : ROW0 + BX + 2, :] = zrows

    await_greetings(0)
    greet(1)

    load_m.wait()
    load_t.wait()
    load_o.wait()
    for rank in range(nz):
        layer = 0
        for o in range(nz):
            layer = jnp.where(order[o] == rank, o, layer)
        at_rank[rank] = layer
    depth_total = BZ * nz
    for c in range(4):
        for m in range(16):
            entry = table[c, m] * (2.0 / depth_total) if c == 3 else table[c, m]
            TB[16 * c + m] = jnp.broadcast_to(entry, (8, 128))

    row = lax.broadcasted_iota(jnp.int32, (128, 128), 0)
    col = lax.broadcasted_iota(jnp.int32, (128, 128), 1)
    row4 = row % 4
    beside = jnp.where(row4 < 2, row4 - 2, row4 + 126)
    beside1 = jnp.where(row4 == 2, -1, jnp.where(row4 == 3, 128, -1000))
    first_y = jnp.where((row == 0) & (col == 0), (gy == 0).astype(f32), 0.0)
    last_y = jnp.where((row == 127) & (col == 127), (gy == ny - 1).astype(f32), 0.0)
    own = jnp.concatenate(
        [
            blur_weight(row - col),
            blur2_weight(row - col) - first_y - last_y,
            slope_weight(row - col) + first_y - last_y,
        ],
        axis=1,
    ).astype(bf16)
    for k in range(3):
        TD[128 * k : 128 * k + 128, :] = own
        TF[128 * k : 128 * k + 128, :] = own[:, 0:128]
    TD[384:512, :] = jnp.concatenate(
        [weight(beside - col) for weight in (blur_weight, blur2_weight, slope_weight)], axis=1
    ).astype(bf16)
    TF[384:512, :] = blur_weight(beside1 - col).astype(bf16)

    @pl.loop(0, BZ)
    def _(z):
        bits = []
        for j in range(4):
            index = M[z, pl.ds(j, 8, stride=4), :]
            bits.append([(index & (1 << k)) != 0 for k in range(4)])
        for c in range(4):
            entries = [TB[16 * c + m] for m in range(16)]
            for j in range(4):
                left = entries
                for k in range(4):
                    left = [jnp.where(bits[j][k], b, a) for a, b in zip(left[::2], left[1::2])]
                LK[z, c, j] = left[0]

    await_greetings(1)
    greet(2)

    def await_cells(group):
        for n, (dz, dx, dy) in enumerate(OFFSETS):
            if (dz != 0) == group:
                @pl.when(there(-dz, -dx, -dy))
                def _():
                    for c in copies(n, dz, dx, dy):
                        c.wait_recv()

    on = lambda cond: cond.astype(f32)
    low_x = jnp.where(sub == 0, on(gx > 0), 1.0)
    high_x = jnp.where(sub == 7, on(gx < nx - 1), 1.0)
    low_z, high_z = on(gz > 0), on(gz < nz - 1)
    def x_mask(cells):
        return [cells[0] * low_x] + cells[1:5] + [cells[5] * high_x]

    js = range(-2, 6)
    js1 = range(-1, 5)

    def x_blur(f, plane, js):
        return blur3([V[f, plane, pl.ds(ROW0 + j, 8, stride=4), :] for j in js])

    def blend(a, b, c):
        return [p + 2.0 * q + r for p, q, r in zip(a, b, c)]

    def put_own(H, base, cells):
        for p in range(len(cells) // 2):
            rows = pl.ds(pl.multiple_of(base + 16 * p, 16), 16)
            parts = split(jnp.concatenate([cells[2 * p], cells[2 * p + 1]], axis=0))
            for k in range(3):
                H[rows, 128 * k : 128 * k + 128] = parts[k]

    await_cells(False)

    def density_step(z, carry):
        before, here = carry[:6], carry[6:]
        after = x_blur(0, z + 3, js)
        put_own(HD, 48 * z + 48, x_mask(blend(before, here, after)))
        return tuple(here) + tuple(after)

    def density_two(i, carry):
        return density_step(2 * i + 2, density_step(2 * i + 1, carry))

    lax.fori_loop(
        0, BZ // 2 - 1, density_two, tuple(x_blur(0, 2, js)) + tuple(x_blur(0, 3, js))
    )

    def field_step(z, carry):
        new = []
        for f in (1, 2, 3):
            before = carry[8 * (f - 1) : 8 * (f - 1) + 4]
            here = carry[8 * (f - 1) + 4 : 8 * f]
            after = x_blur(f, z + 3, js1)
            put_own(HF, 96 * z + 32 * (f - 1), blend(before, here, after))
            new += list(here) + list(after)
        return tuple(new)

    def field_two(i, carry):
        return field_step(2 * i + 2, field_step(2 * i + 1, carry))

    carry = []
    for f in (1, 2, 3):
        carry += x_blur(f, 2, js1) + x_blur(f, 3, js1)
    lax.fori_loop(0, BZ // 2 - 1, field_two, tuple(carry))

    await_cells(True)
    await_greetings(2)
    greet(3)

    u = {p: x_blur(0, p, js) for p in (0, 1, 2, 3, 32, 33, 34, 35)}
    put_own(HD, 0, x_mask([x * low_z for x in blend(u[0], u[1], u[2])]))
    put_own(HD, 48, x_mask(blend(u[1], u[2], u[3])))
    put_own(HD, 48 * BZ, x_mask(blend(u[32], u[33], u[34])))
    put_own(HD, 48 * BZ + 48, x_mask([x * high_z for x in blend(u[33], u[34], u[35])]))
    for f in (1, 2, 3):
        for z in (0, BZ - 1):
            put_own(
                HF, 96 * z + 32 * (f - 1), blend(*[x_blur(f, z + 1 + k, js1) for k in range(3)])
            )

    def packed(s, k, js):
        return [R[s, k, pl.ds(ROW0 + j, 8, stride=4), :] for j in js]

    near = [packed(0, k, js) for k in range(4)]
    far = [packed(1, k, js) for k in range(4)]
    dens = [
        blur3([jnp.where(lane4 < 2, a, b) for a, b in zip(near[k], far[k])]) for k in (0, 2, 3)
    ]
    packed_main, packed_low, packed_high = [], [], []
    for j in range(6):
        u, lo, hi = dens[0][j], dens[1][j], dens[2][j]
        below = jnp.where(lane < 4, lo, pltpu.roll(u, 4, 1))
        above = jnp.where(lane >= 124, hi, pltpu.roll(u, 124, 1))
        mask = low_x if j == 0 else high_x if j == 5 else None
        w = below + 2.0 * u + above
        w_lo = (pltpu.roll(lo, 124, 1) + 2.0 * lo + u) * low_z
        w_hi = (pltpu.roll(hi, 4, 1) + 2.0 * hi + u) * high_z
        if mask is not None:
            w, w_lo, w_hi = w * mask, w_lo * mask, w_hi * mask
        packed_main.append(w)
        packed_low.append(w_lo)
        packed_high.append(w_hi)

    def keep(slot, cells):
        for p in range(len(cells) // 2):
            parts = split(jnp.concatenate([cells[2 * p], cells[2 * p + 1]], axis=0))
            for k in range(3):
                part = parts[k].astype(f32)
                PE[slot, p, k] = pltpu.roll(part, 44 * k, 1) if k else part

    keep(0, packed_main)
    keep(1, packed_low)
    keep(2, packed_high)

    def pair(f, k):
        cells = []
        for a, b in zip(near[k][1:7], far[k][1:7]):
            if f == 1:
                cells.append(jnp.where(lane4 == 2, a, pltpu.roll(b, 3, 1)))
            elif f == 2:
                cells.append(jnp.where(lane4 == 2, pltpu.roll(a, 127, 1), pltpu.roll(b, 2, 1)))
            else:
                cells.append(pltpu.roll(jnp.where(lane4 == 0, a, b), 2, 1))
        return blur3(cells)

    for f in (1, 2, 3):
        main = pair(f, 1 if f == 3 else 0)
        lo, hi = pair(f, 2), pair(f, 3)
        cells = []
        for j in range(4):
            lo_j, hi_j = lo[j], hi[j]
            if f == 3:
                lo_j, hi_j = pltpu.roll(lo_j, 120, 1), pltpu.roll(hi_j, 8, 1)
            below = jnp.where(lane < 4, lo_j, pltpu.roll(main[j], 4, 1))
            above = jnp.where(lane >= 124, hi_j, pltpu.roll(main[j], 124, 1))
            cells.append(below + 2.0 * main[j] + above)
        keep(2 + f, cells)

    group = lax.broadcasted_iota(jnp.int32, (16, 128), 1) // 4

    def put_beside(H, base, slot, pairs, z):
        masks = [group == lax.rem(z + 11 * k, BZ) for k in range(3)]
        for p in range(pairs):
            rows = pl.ds(pl.multiple_of(base + 16 * p, 16), 16)
            beside = jnp.where(masks[2], PE[slot, p, 2], 0.0)
            beside = jnp.where(masks[1], PE[slot, p, 1], beside)
            beside = jnp.where(masks[0], PE[slot, p, 0], beside)
            H[rows, 384:512] = beside.astype(bf16)

    put_beside(HD, 0, 1, 3, 0)
    put_beside(HD, 48 * BZ + 48, 2, 3, BZ - 1)

    def beside_step(z):
        put_beside(HD, 48 * z + 48, 0, 3, z)
        for f in (1, 2, 3):
            put_beside(HF, 96 * z + 32 * (f - 1), 2 + f, 2, z)

    @pl.loop(0, BZ // 2)
    def _(i):
        beside_step(2 * i)
        beside_step(2 * i + 1)

    for k in range(2):
        rows = pl.ds(816 * k, 816)
        DD[rows, :] = jnp.dot(HD[rows, :], TD[...], preferred_element_type=f32)
    for k in range(4):
        rows = pl.ds(768 * k, 768)
        SM[rows, :] = jnp.dot(HF[rows, :], TF[...], preferred_element_type=f32)

    to_exp2 = 3.0 / (64.0 * math.log(2.0))

    def shade_step(z, carry):
        light, depth, red, green, blue = (list(carry[4 * k : 4 * k + 4]) for k in range(5))
        colour = [red, green, blue]

        def part(plane, j, c):
            return DD[pl.ds(pl.multiple_of(48 * (z + plane) + 8 * j, 8), 8), 128 * c : 128 * c + 128]

        by = [[part(p, j, 1) for j in range(6)] for p in range(3)]
        sy = [[part(p, j, 2) for j in range(6)] for p in range(3)]
        along_z = blur3([b - a for a, b in zip(by[0], by[2])])
        across = blend(*by)
        along_y = blur3(blend(*sy))
        for j in range(4):
            g_z, g_x, g_y = along_z[j], across[j + 2] - across[j], along_y[j]
            facing = jnp.abs(2.0 * (g_z + g_y) + g_x)
            norm = g_z * g_z + g_x * g_x + g_y * g_y + 0.0025 * 2048.0 * 2048.0
            shading = 0.3 + 0.4 * facing * lax.rsqrt(norm)
            grown = jnp.exp2(part(1, j + 1, 0) * to_exp2)
            soft = jnp.where(
                grown < 1.0 / 128.0,
                grown * (1.0 + grown * (-0.5 + grown * (1.0 / 3.0))),
                jnp.log(1.0 + grown),
            )
            e = LK[z, 3, j] * soft
            taken = e * (
                1.0 + e * (-0.5 + e * (1.0 / 6.0 + e * (-1.0 / 24.0 + e * (1.0 / 120.0))))
            )
            weight = light[j] * taken
            light[j] = light[j] - weight
            depth[j] = depth[j] + e
            lit = weight * shading
            for c in range(3):
                smooth = SM[pl.ds(pl.multiple_of(96 * z + 32 * c + 8 * j, 8), 8), :]
                tone = 1.0 + 0.5 * jnp.tanh(smooth * (1.0 / 64.0))
                colour[c][j] = colour[c][j] + lit * (LK[z, c, j] * tone)
        return tuple(light + depth + colour[0] + colour[1] + colour[2])

    def shade_two(i, carry):
        return shade_step(2 * i + 1, shade_step(2 * i, carry))

    zero = jnp.zeros((8, 128), f32)
    final = lax.fori_loop(
        0, BZ // 2, shade_two, tuple([jnp.ones((8, 128), f32)] * 4 + [zero] * 16)
    )

    await_greetings(3)

    for c, k in ((0, 2), (1, 3), (2, 4), (3, 1)):
        for j in range(4):
            SB[pl.ds(8 * (j // 2) + 2 * c + j % 2, 8, stride=16), :] = final[4 * k + j]

    def to_peer(k):
        peer = lax.rem(gz + k, nz)
        return pltpu.make_async_remote_copy(
            src_ref=SB.at[pl.ds(pl.multiple_of(peer * 8, 8), 8)],
            dst_ref=RB.at[gz],
            send_sem=a2a_send.at[k],
            recv_sem=a2a_recv.at[k],
            device_id={"gz": peer},
            device_id_type=MESH,
        )

    far_first = sorted(range(1, nz), key=lambda k: (-min(k, nz - k), k))
    for k in far_first:
        to_peer(k).start()
    own = pl.ds(pl.multiple_of(gz * 8, 8), 8)
    RB[gz] = SB[own, :]
    for n, (dz, dx, dy) in enumerate(OFFSETS):
        @pl.when(there(dz, dx, dy))
        def _():
            for c in copies(n, dz, dx, dy):
                c.wait_send()
    for k in far_first:
        to_peer(k).wait_send()
    for k in reversed(far_first):
        to_peer(k).wait_recv()

    total, image = zero, zero
    for rank in range(nz):
        part = RB[at_rank[rank]]
        image = image + jnp.exp(-total) * part
        d = jnp.where(sub >= 6, part, 0.0)
        d = d + pltpu.roll(d, 4, 0)
        total = total + (d + pltpu.roll(d, 2, 0))
    small = total * (
        1.0 + total * (-0.5 + total * (1.0 / 6.0 + total * (-1.0 / 24.0 + total * (1.0 / 120.0))))
    )
    opacity = jnp.where(total < 0.125, small, 1.0 - jnp.exp(-total))
    image = jnp.where(sub >= 6, opacity, image)
    for c in range(4):
        out[c] = image[2 * c : 2 * c + 2, :]


def on_device(fields, material, depth_order, table):
    vmem = lambda *shape: pltpu.VMEM(shape, f32)
    dma = pltpu.SemaphoreType.DMA
    count = len(OFFSETS)
    return pl.pallas_call(
        kernel,
        out_shape=pltpu.VMEM((4, 2, 128), f32),
        in_specs=[pl.BlockSpec(memory_space=pl.ANY)] * 4,
        out_specs=pl.BlockSpec(memory_space=pltpu.VMEM),
        scratch_shapes=[
            vmem(4, BZ + 4, ROWS, 128),
            pltpu.VMEM((BZ, BX, 128), jnp.int32),
            vmem(2, 4, BX, 128),
            vmem(2, 4, ROWS, 128),
            vmem(6, 3, 3, 16, 128),
            pltpu.VMEM((48 * (BZ + 2), 512), bf16),
            pltpu.VMEM((96 * BZ, 512), bf16),
            pltpu.VMEM((512, 384), bf16),
            pltpu.VMEM((512, 128), bf16),
            vmem(48 * (BZ + 2), 384),
            vmem(96 * BZ, 128),
            vmem(BZ, 4, 4, 8, 128),
            vmem(64, 8, 128),
            pltpu.SMEM((4, 16), f32),
            pltpu.SMEM((16,), jnp.int32),
            pltpu.SMEM((16,), jnp.int32),
            vmem(128, 128),
            vmem(16, 8, 128),
            dma((7,)),
            dma((count, 2)),
            dma((count, 2)),
            dma((16,)),
            dma((16,)),
            pltpu.SemaphoreType.REGULAR((4,)),
        ],
        compiler_params=pltpu.CompilerParams(collective_id=0, has_side_effects=True),
    )(fields, material, depth_order, table)


def solution(mesh):
    return jax.shard_map(
        on_device,
        mesh=mesh,
        in_specs=(P(None, "gz", "gx", "gy"), P("gz", "gx", "gy"), P(), P()),
        out_specs=P(None, ("gx", "gz"), "gy"),
        check_vma=False,
    )
```

```python
import math

import jax
import jax.numpy as jnp
from jax import lax
from jax.experimental import pallas as pl
from jax.experimental.pallas import tpu as pltpu
from jax.sharding import PartitionSpec as P

MESH = pl.DeviceIdType.MESH
f32 = jnp.float32
bf16 = jnp.bfloat16

BZ = 32
BX = 32
ROW0 = 8
ROWS = 48

OFFSETS = [
    (dz, dx, dy)
    for dz in (-1, 0, 1)
    for dx in (-1, 0, 1)
    for dy in (-1, 0, 1)
    if (dz, dx, dy) != (0, 0, 0)
]
OFFSETS.sort(key=lambda o: (o[2] == 0, -abs(o[0]) - abs(o[1]) - abs(o[2])))


def z_range(dz, width):
    if dz == 1:
        return pl.ds(BZ - width, width), pl.ds(2 - width, width)
    if dz == -1:
        return pl.ds(0, width), pl.ds(2 + BZ, width)
    return pl.ds(0, BZ), pl.ds(2, BZ)


def x_range(dx, width):
    if dx == 1:
        return pl.ds(BX - width, width), pl.ds(ROW0 - width, width)
    if dx == -1:
        return pl.ds(0, width), pl.ds(ROW0 + BX, width)
    return pl.ds(0, BX), pl.ds(ROW0, BX)


def blur3(cells):
    pairs = [a + b for a, b in zip(cells[:-1], cells[1:])]
    return [a + b for a, b in zip(pairs[:-1], pairs[1:])]


def split(a):
    high = a.astype(bf16)
    rest = a - high.astype(f32)
    middle = rest.astype(bf16)
    return high, middle, (rest - middle.astype(f32)).astype(bf16)


def blur_weight(d):
    return jnp.where(d == 0, 2.0, jnp.where(jnp.abs(d) == 1, 1.0, 0.0))


def blur2_weight(d):
    far = jnp.abs(d)
    return jnp.where(
        far == 0, 6.0, jnp.where(far == 1, 4.0, jnp.where(far == 2, 1.0, 0.0))
    )


def slope_weight(d):
    far = jnp.abs(d)
    size = jnp.where(far == 1, 2.0, jnp.where(far == 2, 1.0, 0.0))
    return jnp.where(d > 0, size, -size)


def kernel(
    fields, material, order_hbm, table_hbm, out,
    V, M, S, R, PE, HD, HF, TD, TF, DD, SM, LK, TB, table, order, at_rank, SB, RB,
    load_sem, send_sem, recv_sem, a2a_send, a2a_recv, greeted,
):
    gz, gx, gy = lax.axis_index("gz"), lax.axis_index("gx"), lax.axis_index("gy")
    nz, nx, ny = lax.axis_size("gz"), lax.axis_size("gx"), lax.axis_size("gy")

    def there(dz, dx, dy):
        ok = None
        for pos, d, n in ((gz, dz, nz), (gx, dx, nx), (gy, dy, ny)):
            if d == 0:
                continue
            this = pos < n - 1 if d == 1 else pos > 0
            ok = this if ok is None else jnp.logical_and(ok, this)
        return ok

    loads = [
        pltpu.make_async_copy(
            fields.at[f], V.at[f, pl.ds(2, BZ), pl.ds(ROW0, BX)], load_sem.at[f]
        )
        for f in range(4)
    ]
    load_m = pltpu.make_async_copy(material, M, load_sem.at[4])
    load_t = pltpu.make_async_copy(table_hbm, table, load_sem.at[5])
    load_o = pltpu.make_async_copy(order_hbm, order, load_sem.at[6])
    loads[0].start()

    barrier = pltpu.get_barrier_semaphore()
    for dz, dx, dy in OFFSETS:
        @pl.when(there(dz, dx, dy))
        def _():
            pl.semaphore_signal(
                barrier,
                inc=1,
                device_id={"gz": gz + dz, "gx": gx + dx, "gy": gy + dy},
                device_id_type=MESH,
            )

    for c in loads[1:]:
        c.start()
    load_m.start()
    load_t.start()
    load_o.start()

    def greet(k):
        for to in (gz + (1 << k), gz - (1 << k)):
            @pl.when(jnp.logical_and(to >= 0, to < nz))
            def _():
                pl.semaphore_signal(
                    greeted.at[k], inc=1, device_id={"gz": to}, device_id_type=MESH
                )

    def await_greetings(k):
        count = (gz >= 1 << k).astype(jnp.int32) + (gz + (1 << k) < nz).astype(jnp.int32)
        pl.semaphore_wait(greeted.at[k], count)

    def span(pos, n):
        return 1 + (pos > 0).astype(jnp.int32) + (pos < n - 1).astype(jnp.int32)

    expected = span(gz, nz) * span(gx, nx) * span(gy, ny) - 1

    lane = lax.broadcasted_iota(jnp.int32, (8, 128), 1)
    sub = lax.broadcasted_iota(jnp.int32, (8, 128), 0)
    lane4 = lane % 4
    lane_z = lane // 4

    acc = [[jnp.zeros((8, 128), f32)] * 4 for _ in range(4)]
    shift0 = (2, 3, 3, 1)
    for f in range(4):
        loads[f].wait()
        for z in range(BZ):
            mask = lane_z == z
            for i in range(4):
                tile = V[f, z + 2, ROW0 + 8 * i : ROW0 + 8 * i + 8, :]
                moved = pltpu.roll(tile, (4 * z + shift0[f]) % 128, 1)
                acc[f][i] = jnp.where(mask, moved, acc[f][i])
    for i in range(4):
        ad, a1, a2, b = (acc[f][i] for f in range(4))
        front = jnp.where(lane4 < 2, ad, jnp.where(lane4 == 2, a1, pltpu.roll(a2, 1, 1)))
        back = jnp.where(
            lane4 >= 2, ad, jnp.where(lane4 == 0, pltpu.roll(a1, 125, 1), pltpu.roll(a2, 126, 1))
        )
        for s, a in ((0, front), (1, back)):
            rows = pl.ds(8 * i, 8)
            S[s, 0, rows, :] = a
            S[s, 1, rows, :] = b
            S[s, 2, rows, :] = jnp.where(
                lane < 4,
                pltpu.roll(a, 4, 1),
                jnp.where(lane < 8, pltpu.roll(a, 12, 1), pltpu.roll(b, 12, 1)),
            )
            S[s, 3, rows, :] = jnp.where(
                lane >= 124,
                pltpu.roll(a, 124, 1),
                jnp.where(lane >= 120, pltpu.roll(a, 116, 1), pltpu.roll(b, 116, 1)),
            )

    def copies(n, dz, dx, dy):
        device = {"gz": gz + dz, "gx": gx + dx, "gy": gy + dy}

        def make(src, dst, k):
            return pltpu.make_async_remote_copy(
                src_ref=src,
                dst_ref=dst,
                send_sem=send_sem.at[n, k],
                recv_sem=recv_sem.at[n, k],
                device_id=device,
                device_id_type=MESH,
            )

        xs2, xd2 = x_range(dx, 2)
        if dy == 0:
            zs2, zd2 = z_range(dz, 2)
            zs1, zd1 = z_range(dz, 1)
            xs1, xd1 = x_range(dx, 1)
            return [
                make(fields.at[0, zs2, xs2], V.at[0, zd2, xd2], 0),
                make(fields.at[pl.ds(1, 3), zs1, xs1], V.at[pl.ds(1, 3), zd1, xd1], 1),
            ]
        side = 0 if dy == 1 else 1
        kinds = {0: pl.ds(0, 2), 1: pl.ds(2, 1), -1: pl.ds(3, 1)}[dz]
        return [make(S.at[side, kinds, xs2], R.at[side, kinds, xd2], 0)]

    pl.semaphore_wait(barrier, expected)
    for n, (dz, dx, dy) in enumerate(OFFSETS):
        @pl.when(there(dz, dx, dy))
        def _():
            for c in copies(n, dz, dx, dy):
                c.start()

    greet(0)

    zrow = jnp.zeros((2, 128), f32)

    @pl.when(gx == 0)
    def _():
        for s in range(2):
            for k in range(4):
                R[s, k, ROW0 - 2 : ROW0, :] = zrow

        @pl.loop(0, BZ + 4)
        def _(z):
            for f in range(4):
                V[f, z, ROW0 - 2 : ROW0, :] = zrow

    @pl.when(gx == nx - 1)
    def _():
        for s in range(2):
            for k in range(4):
                R[s, k, ROW0 + BX : ROW0 + BX + 2, :] = zrow

        @pl.loop(0, BZ + 4)
        def _(z):
            for f in range(4):
                V[f, z, ROW0 + BX : ROW0 + BX + 2, :] = zrow

    zrows = jnp.zeros((BX + 4, 128), f32)

    def clear_planes(planes, kind):
        for s in range(2):
            R[s, kind, ROW0 - 2 : ROW0 + BX + 2, :] = zrows
        for f in range(4):
            for z in planes:
                V[f, z, ROW0 - 2 : ROW0 + BX + 2, :] = zrows

    @pl.when(gz == 0)
    def _():
        clear_planes((0, 1), 2)

    @pl.when(gz == nz - 1)
    def _():
        clear_planes((BZ + 2, BZ + 3), 3)

    for s, edge in ((0, 0), (1, ny - 1)):
        @pl.when(gy == edge)
        def _():
            for k in range(4):
                R[s, k, ROW0 - 2 : ROW0 + BX + 2, :] = zrows

    await_greetings(0)
    greet(1)

    load_m.wait()
    load_t.wait()
    load_o.wait()
    for rank in range(nz):
        layer = 0
        for o in range(nz):
            layer = jnp.where(order[o] == rank, o, layer)
        at_rank[rank] = layer
    depth_total = BZ * nz
    for c in range(4):
        for m in range(16):
            entry = table[c, m] * (2.0 / depth_total) if c == 3 else table[c, m]
            TB[16 * c + m] = jnp.broadcast_to(entry, (8, 128))

    row = lax.broadcasted_iota(jnp.int32, (128, 128), 0)
    col = lax.broadcasted_iota(jnp.int32, (128, 128), 1)
    row4 = row % 4
    beside = jnp.where(row4 < 2, row4 - 2, row4 + 126)
    beside1 = jnp.where(row4 == 2, -1, jnp.where(row4 == 3, 128, -1000))
    first_y = jnp.where((row == 0) & (col == 0), (gy == 0).astype(f32), 0.0)
    last_y = jnp.where((row == 127) & (col == 127), (gy == ny - 1).astype(f32), 0.0)
    own = jnp.concatenate(
        [
            blur_weight(row - col),
            blur2_weight(row - col) - first_y - last_y,
            slope_weight(row - col) + first_y - last_y,
        ],
        axis=1,
    ).astype(bf16)
    for k in range(3):
        TD[128 * k : 128 * k + 128, :] = own
        TF[128 * k : 128 * k + 128, :] = own[:, 0:128]
    TD[384:512, :] = jnp.concatenate(
        [weight(beside - col) for weight in (blur_weight, blur2_weight, slope_weight)], axis=1
    ).astype(bf16)
    TF[384:512, :] = blur_weight(beside1 - col).astype(bf16)

    @pl.loop(0, BZ)
    def _(z):
        bits = []
        for j in range(4):
            index = M[z, pl.ds(j, 8, stride=4), :]
            bits.append([(index & (1 << k)) != 0 for k in range(4)])
        for c in range(4):
            entries = [TB[16 * c + m] for m in range(16)]
            for j in range(4):
                left = entries
                for k in range(4):
                    left = [jnp.where(bits[j][k], b, a) for a, b in zip(left[::2], left[1::2])]
                LK[z, c, j] = left[0]

    await_greetings(1)
    greet(2)

    def await_cells(group):
        for n, (dz, dx, dy) in enumerate(OFFSETS):
            if (dz != 0) == group:
                @pl.when(there(-dz, -dx, -dy))
                def _():
                    for c in copies(n, dz, dx, dy):
                        c.wait_recv()

    on = lambda cond: cond.astype(f32)
    low_x = jnp.where(sub == 0, on(gx > 0), 1.0)
    high_x = jnp.where(sub == 7, on(gx < nx - 1), 1.0)
    low_z, high_z = on(gz > 0), on(gz < nz - 1)
    def x_mask(cells):
        return [cells[0] * low_x] + cells[1:5] + [cells[5] * high_x]

    js = range(-2, 6)
    js1 = range(-1, 5)

    def x_blur(f, plane, js):
        return blur3([V[f, plane, pl.ds(ROW0 + j, 8, stride=4), :] for j in js])

    def blend(a, b, c):
        return [p + 2.0 * q + r for p, q, r in zip(a, b, c)]

    def put_own(H, base, cells):
        for p in range(len(cells) // 2):
            rows = pl.ds(pl.multiple_of(base + 16 * p, 16), 16)
            parts = split(jnp.concatenate([cells[2 * p], cells[2 * p + 1]], axis=0))
            for k in range(3):
                H[rows, 128 * k : 128 * k + 128] = parts[k]

    await_cells(False)

    def density_step(z, carry):
        before, here = carry[:6], carry[6:]
        after = x_blur(0, z + 3, js)
        put_own(HD, 48 * z + 48, x_mask(blend(before, here, after)))
        return tuple(here) + tuple(after)

    def density_two(i, carry):
        return density_step(2 * i + 2, density_step(2 * i + 1, carry))

    lax.fori_loop(
        0, BZ // 2 - 1, density_two, tuple(x_blur(0, 2, js)) + tuple(x_blur(0, 3, js))
    )

    def field_step(z, carry):
        new = []
        for f in (1, 2, 3):
            before = carry[8 * (f - 1) : 8 * (f - 1) + 4]
            here = carry[8 * (f - 1) + 4 : 8 * f]
            after = x_blur(f, z + 3, js1)
            put_own(HF, 96 * z + 32 * (f - 1), blend(before, here, after))
            new += list(here) + list(after)
        return tuple(new)

    def field_two(i, carry):
        return field_step(2 * i + 2, field_step(2 * i + 1, carry))

    carry = []
    for f in (1, 2, 3):
        carry += x_blur(f, 2, js1) + x_blur(f, 3, js1)
    lax.fori_loop(0, BZ // 2 - 1, field_two, tuple(carry))

    await_cells(True)
    await_greetings(2)
    greet(3)

    u = {p: x_blur(0, p, js) for p in (0, 1, 2, 3, 32, 33, 34, 35)}
    put_own(HD, 0, x_mask([x * low_z for x in blend(u[0], u[1], u[2])]))
    put_own(HD, 48, x_mask(blend(u[1], u[2], u[3])))
    put_own(HD, 48 * BZ, x_mask(blend(u[32], u[33], u[34])))
    put_own(HD, 48 * BZ + 48, x_mask([x * high_z for x in blend(u[33], u[34], u[35])]))
    for f in (1, 2, 3):
        for z in (0, BZ - 1):
            put_own(
                HF, 96 * z + 32 * (f - 1), blend(*[x_blur(f, z + 1 + k, js1) for k in range(3)])
            )

    def packed(s, k, js):
        return [R[s, k, pl.ds(ROW0 + j, 8, stride=4), :] for j in js]

    near = [packed(0, k, js) for k in range(4)]
    far = [packed(1, k, js) for k in range(4)]
    dens = [
        blur3([jnp.where(lane4 < 2, a, b) for a, b in zip(near[k], far[k])]) for k in (0, 2, 3)
    ]
    packed_main, packed_low, packed_high = [], [], []
    for j in range(6):
        u, lo, hi = dens[0][j], dens[1][j], dens[2][j]
        below = jnp.where(lane < 4, lo, pltpu.roll(u, 4, 1))
        above = jnp.where(lane >= 124, hi, pltpu.roll(u, 124, 1))
        mask = low_x if j == 0 else high_x if j == 5 else None
        w = below + 2.0 * u + above
        w_lo = (pltpu.roll(lo, 124, 1) + 2.0 * lo + u) * low_z
        w_hi = (pltpu.roll(hi, 4, 1) + 2.0 * hi + u) * high_z
        if mask is not None:
            w, w_lo, w_hi = w * mask, w_lo * mask, w_hi * mask
        packed_main.append(w)
        packed_low.append(w_lo)
        packed_high.append(w_hi)

    def keep(slot, cells):
        for p in range(len(cells) // 2):
            parts = split(jnp.concatenate([cells[2 * p], cells[2 * p + 1]], axis=0))
            for k in range(3):
                part = parts[k].astype(f32)
                PE[slot, p, k] = pltpu.roll(part, 44 * k, 1) if k else part

    keep(0, packed_main)
    keep(1, packed_low)
    keep(2, packed_high)

    def pair(f, k):
        cells = []
        for a, b in zip(near[k][1:7], far[k][1:7]):
            if f == 1:
                cells.append(jnp.where(lane4 == 2, a, pltpu.roll(b, 3, 1)))
            elif f == 2:
                cells.append(jnp.where(lane4 == 2, pltpu.roll(a, 127, 1), pltpu.roll(b, 2, 1)))
            else:
                cells.append(pltpu.roll(jnp.where(lane4 == 0, a, b), 2, 1))
        return blur3(cells)

    for f in (1, 2, 3):
        main = pair(f, 1 if f == 3 else 0)
        lo, hi = pair(f, 2), pair(f, 3)
        cells = []
        for j in range(4):
            lo_j, hi_j = lo[j], hi[j]
            if f == 3:
                lo_j, hi_j = pltpu.roll(lo_j, 120, 1), pltpu.roll(hi_j, 8, 1)
            below = jnp.where(lane < 4, lo_j, pltpu.roll(main[j], 4, 1))
            above = jnp.where(lane >= 124, hi_j, pltpu.roll(main[j], 124, 1))
            cells.append(below + 2.0 * main[j] + above)
        keep(2 + f, cells)

    group = lax.broadcasted_iota(jnp.int32, (16, 128), 1) // 4

    def put_beside(H, base, slot, pairs, z):
        masks = [group == lax.rem(z + 11 * k, BZ) for k in range(3)]
        for p in range(pairs):
            rows = pl.ds(pl.multiple_of(base + 16 * p, 16), 16)
            beside = jnp.where(masks[2], PE[slot, p, 2], 0.0)
            beside = jnp.where(masks[1], PE[slot, p, 1], beside)
            beside = jnp.where(masks[0], PE[slot, p, 0], beside)
            H[rows, 384:512] = beside.astype(bf16)

    put_beside(HD, 0, 1, 3, 0)
    put_beside(HD, 48 * BZ + 48, 2, 3, BZ - 1)

    def beside_step(z):
        put_beside(HD, 48 * z + 48, 0, 3, z)
        for f in (1, 2, 3):
            put_beside(HF, 96 * z + 32 * (f - 1), 2 + f, 2, z)

    @pl.loop(0, BZ // 2)
    def _(i):
        beside_step(2 * i)
        beside_step(2 * i + 1)

    for k in range(2):
        rows = pl.ds(816 * k, 816)
        DD[rows, :] = jnp.dot(HD[rows, :], TD[...], preferred_element_type=f32)
    for k in range(4):
        rows = pl.ds(768 * k, 768)
        SM[rows, :] = jnp.dot(HF[rows, :], TF[...], preferred_element_type=f32)

    to_exp2 = 3.0 / (64.0 * math.log(2.0))

    def shade_step(z, carry):
        light, depth, red, green, blue = (list(carry[4 * k : 4 * k + 4]) for k in range(5))
        colour = [red, green, blue]

        def part(plane, j, c):
            return DD[pl.ds(pl.multiple_of(48 * (z + plane) + 8 * j, 8), 8), 128 * c : 128 * c + 128]

        by = [[part(p, j, 1) for j in range(6)] for p in range(3)]
        sy = [[part(p, j, 2) for j in range(6)] for p in range(3)]
        along_z = blur3([b - a for a, b in zip(by[0], by[2])])
        across = blend(*by)
        along_y = blur3(blend(*sy))
        for j in range(4):
            g_z, g_x, g_y = along_z[j], across[j + 2] - across[j], along_y[j]
            facing = jnp.abs(2.0 * (g_z + g_y) + g_x)
            norm = g_z * g_z + g_x * g_x + g_y * g_y + 0.0025 * 2048.0 * 2048.0
            shading = 0.3 + 0.4 * facing * lax.rsqrt(norm)
            grown = jnp.exp2(part(1, j + 1, 0) * to_exp2)
            soft = jnp.where(
                grown < 1.0 / 128.0,
                grown * (1.0 + grown * (-0.5 + grown * (1.0 / 3.0))),
                jnp.log(1.0 + grown),
            )
            e = LK[z, 3, j] * soft
            taken = e * (
                1.0 + e * (-0.5 + e * (1.0 / 6.0 + e * (-1.0 / 24.0 + e * (1.0 / 120.0))))
            )
            weight = light[j] * taken
            light[j] = light[j] - weight
            depth[j] = depth[j] + e
            lit = weight * shading
            for c in range(3):
                smooth = SM[pl.ds(pl.multiple_of(96 * z + 32 * c + 8 * j, 8), 8), :]
                tone = 1.0 + 0.5 * jnp.tanh(smooth * (1.0 / 64.0))
                colour[c][j] = colour[c][j] + lit * (LK[z, c, j] * tone)
        return tuple(light + depth + colour[0] + colour[1] + colour[2])

    def shade_four(i, carry):
        for k in range(4):
            carry = shade_step(4 * i + k, carry)
        return carry

    zero = jnp.zeros((8, 128), f32)
    final = lax.fori_loop(
        0, BZ // 4, shade_four, tuple([jnp.ones((8, 128), f32)] * 4 + [zero] * 16)
    )

    await_greetings(3)

    for c, k in ((0, 2), (1, 3), (2, 4), (3, 1)):
        for j in range(4):
            SB[pl.ds(8 * (j // 2) + 2 * c + j % 2, 8, stride=16), :] = final[4 * k + j]

    def to_peer(k):
        peer = lax.rem(gz + k, nz)
        return pltpu.make_async_remote_copy(
            src_ref=SB.at[pl.ds(pl.multiple_of(peer * 8, 8), 8)],
            dst_ref=RB.at[gz],
            send_sem=a2a_send.at[k],
            recv_sem=a2a_recv.at[k],
            device_id={"gz": peer},
            device_id_type=MESH,
        )

    far_first = sorted(range(1, nz), key=lambda k: (-min(k, nz - k), k))
    for k in far_first:
        to_peer(k).start()
    own = pl.ds(pl.multiple_of(gz * 8, 8), 8)
    RB[gz] = SB[own, :]
    for n, (dz, dx, dy) in enumerate(OFFSETS):
        @pl.when(there(dz, dx, dy))
        def _():
            for c in copies(n, dz, dx, dy):
                c.wait_send()
    for k in far_first:
        to_peer(k).wait_send()
    for k in reversed(far_first):
        to_peer(k).wait_recv()

    total, image = zero, zero
    for rank in range(nz):
        part = RB[at_rank[rank]]
        image = image + jnp.exp(-total) * part
        d = jnp.where(sub >= 6, part, 0.0)
        d = d + pltpu.roll(d, 4, 0)
        total = total + (d + pltpu.roll(d, 2, 0))
    small = total * (
        1.0 + total * (-0.5 + total * (1.0 / 6.0 + total * (-1.0 / 24.0 + total * (1.0 / 120.0))))
    )
    opacity = jnp.where(total < 0.125, small, 1.0 - jnp.exp(-total))
    image = jnp.where(sub >= 6, opacity, image)
    for c in range(4):
        out[c] = image[2 * c : 2 * c + 2, :]


def on_device(fields, material, depth_order, table):
    vmem = lambda *shape: pltpu.VMEM(shape, f32)
    dma = pltpu.SemaphoreType.DMA
    count = len(OFFSETS)
    return pl.pallas_call(
        kernel,
        out_shape=pltpu.VMEM((4, 2, 128), f32),
        in_specs=[pl.BlockSpec(memory_space=pl.ANY)] * 4,
        out_specs=pl.BlockSpec(memory_space=pltpu.VMEM),
        scratch_shapes=[
            vmem(4, BZ + 4, ROWS, 128),
            pltpu.VMEM((BZ, BX, 128), jnp.int32),
            vmem(2, 4, BX, 128),
            vmem(2, 4, ROWS, 128),
            vmem(6, 3, 3, 16, 128),
            pltpu.VMEM((48 * (BZ + 2), 512), bf16),
            pltpu.VMEM((96 * BZ, 512), bf16),
            pltpu.VMEM((512, 384), bf16),
            pltpu.VMEM((512, 128), bf16),
            vmem(48 * (BZ + 2), 384),
            vmem(96 * BZ, 128),
            vmem(BZ, 4, 4, 8, 128),
            vmem(64, 8, 128),
            pltpu.SMEM((4, 16), f32),
            pltpu.SMEM((16,), jnp.int32),
            pltpu.SMEM((16,), jnp.int32),
            vmem(128, 128),
            vmem(16, 8, 128),
            dma((7,)),
            dma((count, 2)),
            dma((count, 2)),
            dma((16,)),
            dma((16,)),
            pltpu.SemaphoreType.REGULAR((4,)),
        ],
        compiler_params=pltpu.CompilerParams(collective_id=0, has_side_effects=True),
    )(fields, material, depth_order, table)


def solution(mesh):
    return jax.shard_map(
        on_device,
        mesh=mesh,
        in_specs=(P(None, "gz", "gx", "gy"), P("gz", "gx", "gy"), P(), P()),
        out_specs=P(None, ("gx", "gz"), "gy"),
        check_vma=False,
    )
```
